32 devices in a mesh: grp: 2 (over y), seq: 16 (over z, x, core).
Axes of the slice: x: 2, y: 2, z: 4, core: 2. Of those that a mesh axis runs over, the one named last changes fastest.
Arguments:
- streams: bfloat16 [3, 4096, 4096], P(None, ('grp', 'seq')), parts along dimension 1, may hold values from -12 to 12
- long_filter: bfloat16 [4096, 2048], P('seq'), may hold values from -1 to 1
- gain: bfloat16 [4096], replicated, may hold values from 0.099609375 to 1.8984375
- unembed: bfloat16 [4096, 512], P('seq'), may hold values from -8 to 8
- offsets: int32 [32], P('grp'), parts along dimension 0, may hold values from 0 to 127
- ref_ids: int32 [32], P(('grp', 'seq')), parts along dimension 0, may hold values from 0 to 511
- alt_ids: int32 [32], P(('grp', 'seq')), parts along dimension 0, may hold values from 0 to 511
Outputs:
- mixed: bfloat16 [4096, 4096], P(('grp', 'seq')), parts along dimension 0
- scores: float32 [2, 32], P(None, ('grp', 'seq')), parts along dimension 1
The draws below stay inside these ranges and needn't reach their ends.
There are 2 independent parts, one for each index of `grp`. The reference program is written for one: setup_inputs(seed, part) draws one part's arguments, and reference() takes and returns one part's arrays. A program takes and returns all parts, laid end to end along the dimension named above; an argument that names none is the same for every part. Nothing has to cross between parts.
All inputs are finite; a program needn't handle non-finite values.
Results may differ from the reference program's by a relative error of at most 0.0057.
Values may be sent and summed in bfloat16 or wider, within the bound.
A program may use at most 128 MiB of HBM per device.

```python
import math
import jax
import jax.numpy as jnp
from jax import lax

D = 4096
V = 512
TOK_DEV = 128
VARS_DEV = 1
WINDOW_LENGTH = 2048
NVAR = 16


def draw_streams(key, part):
    random_subkey_list = jax.random.split(key, 1)
    noise_all = jnp.clip(jax.random.normal(random_subkey_list[0], (3, WINDOW_LENGTH, D), jnp.float32), -4.0, 4.0)
    channel_ramp = jnp.arange(D, dtype=jnp.float32) / max(D - 1, 1)
    gate_scale = 1.0 + 2.0 * channel_ramp
    gate_part = noise_all[0] * gate_scale[None, :]
    stacked = jnp.stack([gate_part, noise_all[1], noise_all[2]])
    return jnp.clip(stacked, -12.0, 12.0).astype(jnp.bfloat16)


def draw_long_filter(key, part):
    random_subkey_list = jax.random.split(key, 6)
    noise_part = jnp.clip(jax.random.normal(random_subkey_list[0], (D, WINDOW_LENGTH), jnp.float32), -4.0, 4.0)
    chooser = jax.random.uniform(random_subkey_list[1], (D,), jnp.float32)
    fast_share = 0.5
    fast_tau = jax.random.uniform(random_subkey_list[2], (D,), jnp.float32, minval=10.0, maxval=17.0)
    slow_tau = WINDOW_LENGTH * jax.random.uniform(random_subkey_list[3], (D,), jnp.float32, minval=2.0, maxval=4.0)
    decay_constant = jnp.where(chooser < fast_share, fast_tau, slow_tau)
    step_positions = jnp.arange(WINDOW_LENGTH, dtype=jnp.float32)
    spike_position = jax.random.randint(random_subkey_list[4], (3,), 1, WINDOW_LENGTH).astype(jnp.float32)
    spike_retained = jax.random.uniform(random_subkey_list[5], (3,), jnp.float32, minval=0.55, maxval=0.8)
    spike_multiplier = jnp.prod(jnp.where(step_positions[None, :] >= spike_position[:, None], spike_retained[:, None], 1.0), axis=0)
    decay_envelope = jnp.exp(-step_positions[None, :] / decay_constant[:, None]) * spike_multiplier[None, :]
    scaled = decay_envelope / jnp.sqrt(jnp.sum(decay_envelope * decay_envelope, axis=1, keepdims=True))
    return jnp.clip(noise_part * scaled, -1.0, 1.0).astype(jnp.bfloat16)


def draw_unembed(key, part):
    random_subkey_list = jax.random.split(key, 1)
    drawn_part = jnp.clip(jax.random.normal(random_subkey_list[0], (D, V), jnp.float32), -5.0, 5.0) * (3.0 / math.sqrt(D))
    table = drawn_part
    return jnp.clip(table, -8.0, 8.0).astype(jnp.bfloat16)


def place_ends(entries, rng, low, high):
    spot = [jax.random.randint(jax.random.fold_in(rng, axis), (), 0, length) for axis, length in enumerate(entries.shape)]
    longest = entries.shape.index(max(entries.shape))
    neighbour = spot[:longest] + [(spot[longest] + 1) % entries.shape[longest]] + spot[longest + 1:]
    return entries.at[tuple(spot)].set(low).at[tuple(neighbour)].set(high)


def setup_inputs(seed: int = 0, part: int = 0) -> dict:
    arg_keys = jax.random.split(jax.random.key(seed), 8)
    part_keys = jax.random.split(jax.random.fold_in(arg_keys[7], part), 8)
    streams = draw_streams(jax.random.fold_in(jax.random.fold_in(arg_keys[7], part), 71), part)
    long_filter = draw_long_filter(jax.random.fold_in(arg_keys[7], 71), part)
    gain = jnp.clip(1.0 + 0.18 * jax.random.normal(arg_keys[2], (D,), jnp.float32), 0.099609375, 1.8984375).astype(jnp.bfloat16)
    unembed = draw_unembed(jax.random.fold_in(arg_keys[7], 71), part)
    offsets = place_ends(jax.random.randint(part_keys[4], (NVAR,), 0, TOK_DEV // VARS_DEV), jax.random.fold_in(part_keys[4], 1), 0, (TOK_DEV // VARS_DEV) - 1).astype(jnp.int32)
    ref_ids = place_ends(jax.random.randint(part_keys[5], (NVAR,), 0, V), jax.random.fold_in(part_keys[5], 1), 0, V - 1).astype(jnp.int32)
    alt_ids = place_ends(jax.random.randint(part_keys[6], (NVAR,), 0, V), jax.random.fold_in(part_keys[6], 1), 0, V - 1).astype(jnp.int32)
    return dict(streams=streams, long_filter=long_filter, gain=gain, unembed=unembed, offsets=offsets, ref_ids=ref_ids, alt_ids=alt_ids)


norm_eps = 1e-06

def filter_block(pair):
    signal, kernel = pair
    padded_len = 2 * signal.shape[1]
    spectrum = jnp.fft.rfft(signal, n=padded_len, axis=1) * jnp.fft.rfft(kernel, n=padded_len, axis=1)
    return jnp.fft.irfft(spectrum, n=padded_len, axis=1)[:, :signal.shape[1]]

def reference(streams, long_filter, gain, unembed, offsets, ref_ids, alt_ids):
    products = (streams[1].astype(jnp.float32) * streams[2].astype(jnp.float32)).astype(jnp.bfloat16)
    blocks = D // 128
    signal = products.astype(jnp.float32).T.reshape(blocks, 128, WINDOW_LENGTH)
    kernel = long_filter.astype(jnp.float32).reshape(blocks, 128, WINDOW_LENGTH)
    convolved = lax.map(filter_block, (signal, kernel)).reshape(D, WINDOW_LENGTH).T
    filtered = convolved.astype(jnp.bfloat16)
    mixed = (streams[0].astype(jnp.float32) * filtered.astype(jnp.float32)).astype(jnp.bfloat16)
    positions = jnp.arange(NVAR, dtype=jnp.int32) * (WINDOW_LENGTH // NVAR) + offsets.astype(jnp.int32)
    rows = mixed[positions]
    weighted = (rows.astype(jnp.float32) * gain.astype(jnp.float32)[None, :]).astype(jnp.bfloat16)
    raw = jnp.dot(weighted, unembed, preferred_element_type=jnp.float32)
    squares = lax.optimization_barrier(jnp.sum(jnp.square(rows.astype(jnp.float32)), axis=1))
    logits = raw * lax.rsqrt(squares / D + norm_eps)[:, None]
    largest = lax.optimization_barrier(jnp.max(logits, axis=1))
    log_total = largest + jnp.log(lax.optimization_barrier(jnp.sum(jnp.exp(logits - largest[:, None]), axis=1)))
    vocab_ids = jnp.arange(V, dtype=jnp.int32)
    ref_logit = lax.optimization_barrier(jnp.sum(jnp.where(vocab_ids[None, :] == ref_ids[:, None], logits, 0.0), axis=1))
    alt_logit = lax.optimization_barrier(jnp.sum(jnp.where(vocab_ids[None, :] == alt_ids[:, None], logits, 0.0), axis=1))
    scores = jnp.stack([ref_logit - log_total, alt_logit - ref_logit])
    return (mixed, scores)
```

```python
import functools
import math

import jax
import jax.numpy as jnp
import numpy as np
from jax import lax
from jax.experimental import pallas as pl
from jax.experimental.pallas import tpu as pltpu
from jax.sharding import PartitionSpec as P

norm_eps = 1e-06
highest = lax.Precision.HIGHEST
LANES = 128
BLOCK = 256
PLANES = 4
MESH = pl.DeviceIdType.MESH


def angle_pair(left_count, right_count, period):
    product = (
        jnp.arange(left_count, dtype=jnp.int32)[:, None]
        * jnp.arange(right_count, dtype=jnp.int32)[None, :]
        % period
    )
    theta = product.astype(jnp.float32) * (2.0 * math.pi / period)
    return (jnp.cos(theta), jnp.sin(theta))


def forward_spectrum(signal, outer_cos, outer_sin, twist_cos, twist_sin, inner_cos, inner_sin):
    first_re = jnp.einsum("kn,cnm->ckm", outer_cos, signal, precision=highest)
    first_im = -jnp.einsum("kn,cnm->ckm", outer_sin, signal, precision=highest)
    middle_re = first_re * twist_cos + first_im * twist_sin
    middle_im = first_im * twist_cos - first_re * twist_sin
    spec_re = jnp.einsum("ckn,nm->ckm", middle_re, inner_cos, precision=highest) + jnp.einsum(
        "ckn,nm->ckm", middle_im, inner_sin, precision=highest
    )
    spec_im = jnp.einsum("ckn,nm->ckm", middle_im, inner_cos, precision=highest) - jnp.einsum(
        "ckn,nm->ckm", middle_re, inner_sin, precision=highest
    )
    return (spec_re, spec_im)


def causal_filter(signal_rows, kernel_rows, n_blocks):
    channels, length = signal_rows.shape
    half_rows = length // n_blocks
    outer_len = 2 * half_rows
    period = 2 * length
    outer_cos, outer_sin = angle_pair(outer_len, half_rows, outer_len)
    twist_cos, twist_sin = angle_pair(outer_len, n_blocks, period)
    inner_cos, inner_sin = angle_pair(n_blocks, n_blocks, n_blocks)
    tables = (outer_cos, outer_sin, twist_cos, twist_sin, inner_cos, inner_sin)
    signal_re, signal_im = forward_spectrum(
        signal_rows.astype(jnp.float32).reshape(channels, half_rows, n_blocks), *tables
    )
    kernel_re, kernel_im = forward_spectrum(
        kernel_rows.astype(jnp.float32).reshape(channels, half_rows, n_blocks), *tables
    )
    joint_re = signal_re * kernel_re - signal_im * kernel_im
    joint_im = signal_re * kernel_im + signal_im * kernel_re
    back_re = jnp.einsum("ckn,nm->ckm", joint_re, inner_cos, precision=highest) - jnp.einsum(
        "ckn,nm->ckm", joint_im, inner_sin, precision=highest
    )
    back_im = jnp.einsum("ckn,nm->ckm", joint_im, inner_cos, precision=highest) + jnp.einsum(
        "ckn,nm->ckm", joint_re, inner_sin, precision=highest
    )
    turned_re = back_re * twist_cos - back_im * twist_sin
    turned_im = back_im * twist_cos + back_re * twist_sin
    result = jnp.einsum("kn,ckm->cnm", outer_cos, turned_re, precision=highest) - jnp.einsum(
        "kn,ckm->cnm", outer_sin, turned_im, precision=highest
    )
    return (result / period).reshape(channels, length)


def variant_scores(raw_terms, square_terms, model_width, ref_ids, alt_ids):
    logits = raw_terms * lax.rsqrt(square_terms / model_width + norm_eps)[:, None]
    largest = jnp.max(logits, axis=1)
    log_total = largest + jnp.log(jnp.sum(jnp.exp(logits - largest[:, None]), axis=1))
    vocab_ids = jnp.arange(logits.shape[1], dtype=jnp.int32)
    ref_logit = jnp.sum(jnp.where(vocab_ids[None, :] == ref_ids[:, None], logits, 0.0), axis=1)
    alt_logit = jnp.sum(jnp.where(vocab_ids[None, :] == alt_ids[:, None], logits, 0.0), axis=1)
    return jnp.stack([ref_logit - log_total, alt_logit - ref_logit])


def pick_local(mixed, offsets, my_index, vars_dev):
    stride_rows = mixed.shape[0] // vars_dev
    local_offsets = lax.dynamic_slice_in_dim(offsets, my_index * vars_dev, vars_dev)
    row_index = jnp.arange(vars_dev, dtype=jnp.int32) * stride_rows + local_offsets
    return mixed[row_index]


def plain_shards(streams, long_filter, gain, unembed, offsets, ref_ids, alt_ids):
    n_devices = lax.axis_size("seq")
    my_index = lax.axis_index("seq")
    tok_rows = streams.shape[1]
    model_width = streams.shape[2]
    group_width = model_width // n_devices
    length = tok_rows * n_devices
    vars_dev = ref_ids.shape[0]
    products = (streams[1].astype(jnp.float32) * streams[2].astype(jnp.float32)).astype(
        jnp.bfloat16
    )
    split_view = products.reshape(tok_rows, n_devices, group_width)
    moved_prod = lax.all_to_all(split_view, "seq", split_axis=1, concat_axis=0, tiled=True)
    convolved = causal_filter(moved_prod.reshape(length, group_width).T, long_filter, n_devices)
    filtered_back = convolved.astype(jnp.bfloat16).T.reshape(length, 1, group_width)
    filtered = lax.all_to_all(
        filtered_back, "seq", split_axis=0, concat_axis=1, tiled=True
    ).reshape(tok_rows, model_width)
    mixed = (streams[0].astype(jnp.float32) * filtered.astype(jnp.float32)).astype(jnp.bfloat16)
    picked = pick_local(mixed, offsets, my_index, vars_dev)
    weighted = (picked.astype(jnp.float32) * gain.astype(jnp.float32)[None, :]).astype(jnp.bfloat16)
    square_terms = jnp.sum(jnp.square(picked.astype(jnp.float32)), axis=1)
    raw_terms = jnp.dot(
        weighted,
        lax.all_gather(unembed, "seq", axis=0, tiled=True),
        preferred_element_type=jnp.float32,
    )
    scores = variant_scores(raw_terms, square_terms, model_width, ref_ids, alt_ids)
    return (mixed, scores)


def block_tables(block):
    freq = 2 * np.arange(block)[:, None] + 1
    time = np.arange(block)[None, :]
    period = 4 * block
    theta = (freq * time % period) * (2.0 * np.pi / period)
    forward = np.concatenate([np.cos(theta), -np.sin(theta)], axis=0)
    theta = (freq * (time + block) % period).T * (2.0 * np.pi / period)
    inverse = np.concatenate([np.cos(theta), -np.sin(theta)], axis=1) / block
    split = []
    for table in (forward, inverse):
        high = table.astype(np.float32).astype(jnp.bfloat16)
        low = (table - high.astype(np.float64)).astype(np.float32).astype(jnp.bfloat16)
        split += [high, low]
    return split


def dot32(left, right):
    return jnp.dot(left, right, preferred_element_type=jnp.float32)


def layer_kernel(
    cfg,
    off_hbm, ref_id_ref, alt_id_ref,
    streams_hbm, filter_hbm, gain_hbm, unembed_hbm,
    fwd_hi_hbm, fwd_lo_hbm, inv_hi_hbm, inv_lo_hbm,
    mixed_ref, scores_ref,
    off_ref,
    streams_ref, filter_ref, gain_ref, unembed_ref,
    fwd_hi_ref, fwd_lo_ref, inv_hi_ref, inv_lo_ref,
    prod_out, prod_in, filt_out, filt_in, spec, taps,
    gate_out, gate_in, part_out, part_in, gain_rows,
    ps_sem, pr_sem, fs_sem, fr_sem, gs_sem, gr_sem, qs_sem, qr_sem, in_sem,
    side_in, mids_in, far_side_in,
):
    n, halves, rows, width, vocab, model_width = cfg
    me = lax.axis_index("seq")
    n_blocks = n * rows // BLOCK
    per_block = BLOCK // rows
    group = halves * width

    barrier = pltpu.get_barrier_semaphore()

    team = n // PLANES
    plane = me // team
    spot = lax.rem(me, team)
    is_mid = lax.rem((plane + 1) // 2, 2)
    is_outer = 1 - is_mid

    def flip(value, step, size):
        bit, out = 1, 0
        while bit < size:
            out = out + bit * lax.rem(value // bit + step // bit, 2)
            bit *= 2
        return out

    def peer_at(plane_step, spot_step):
        return flip(plane, plane_step, PLANES) * team + flip(spot, spot_step, team)

    def far_step(k):
        return 3 - k + jnp.where(k < 2, is_mid * (2 * k - 1), 0)

    def partner(k):
        return peer_at(far_step((k - 1) // team), team - 1 - lax.rem(k - 1, team))

    def signal(sem, peer):
        pl.semaphore_signal(sem, inc=1, device_id={"seq": peer}, device_id_type=MESH)

    def greet(plane_step, first):
        for k in range(first, team):
            signal(barrier, peer_at(plane_step, k))

    @pl.when(is_mid == 1)
    def _():
        greet(3, 0)
        greet(1, 0)

    greet(0, 1)

    def early_step(k):
        mid_steps, outer_steps = (3, 0, 1, 2), (1, 0, 2, 3)
        return outer_steps[k] + (mid_steps[k] - outer_steps[k]) * is_mid

    def plane_stream(k):
        share = model_width // PLANES
        first = pl.multiple_of(flip(plane, early_step(k), PLANES) * share, LANES)
        part = (pl.ds(1, 2), slice(None), pl.ds(first, share))
        return pltpu.make_async_copy(streams_hbm.at[part], streams_ref.at[part], in_sem.at[k])

    def load(src, dst, sem):
        return pltpu.make_async_copy(src, dst, in_sem.at[sem])

    plane_loads = [plane_stream(k) for k in range(PLANES)]
    gate_load = load(streams_hbm.at[0], streams_ref.at[0], 4)
    off_load = load(off_hbm, off_ref, 5)
    tap_loads = [
        load(filter_hbm, filter_ref, 6),
        load(fwd_hi_hbm, fwd_hi_ref, 7),
        load(fwd_lo_hbm, fwd_lo_ref, 8),
    ]
    late_loads = [
        load(inv_hi_hbm, inv_hi_ref, 9),
        load(inv_lo_hbm, inv_lo_ref, 10),
        load(gain_hbm, gain_ref, 11),
        load(unembed_hbm, unembed_ref, 12),
    ]
    for each in plane_loads + [off_load, gate_load] + tap_loads + late_loads:
        each.start()

    def lanes(owner, half):
        return pl.ds(pl.multiple_of(owner * group + half * width, LANES), width)

    def product(owner, half):
        cols = lanes(owner, half)
        left = streams_ref[1, :, cols].astype(jnp.float32)
        right = streams_ref[2, :, cols].astype(jnp.float32)
        return (left * right).astype(jnp.bfloat16)

    def copy(src, dst, send_sem, recv_sem, peer):
        return pltpu.make_async_remote_copy(
            src_ref=src, dst_ref=dst, send_sem=send_sem, recv_sem=recv_sem,
            device_id={"seq": peer}, device_id_type=MESH,
        )

    def prod_copy(half, peer, slot):
        return copy(
            prod_out.at[half, peer], prod_in.at[half, slot],
            ps_sem.at[half, peer], pr_sem.at[half, slot], peer,
        )

    def filt_copy(half, peer, slot):
        return copy(
            filt_out.at[half, peer], filt_in.at[half, slot],
            fs_sem.at[half, peer], fr_sem.at[half, slot], peer,
        )

    def gate_copy(peer, slot):
        return copy(gate_out.at[peer], gate_in.at[slot], gs_sem.at[peer], gr_sem.at[slot], peer)

    def part_copy(peer, slot):
        return copy(part_out.at[peer], part_in.at[slot], qs_sem.at[peer], qr_sem.at[slot], peer)

    def over_peers(body):
        def step(k, carry):
            body(partner(k))
            return carry

        lax.fori_loop(1, n, step, 0)

    def make_plane(half, plane_step):
        def step(k, carry):
            owner = peer_at(plane_step, k)
            prod_out[half, owner] = product(owner, half)
            return carry

        lax.fori_loop(0, team, step, 0)

    def send_plane(half, plane_step, first):
        def step(k, carry):
            prod_copy(half, peer_at(plane_step, k), me).start()
            return carry

        lax.fori_loop(first, team, step, 0)

    @pl.when(is_outer == 1)
    def _():
        pl.semaphore_wait(barrier, 2 * team - 1)
        for k in range(team):
            signal(side_in, peer_at(1, k))

    plane_loads[0].wait()
    make_plane(0, early_step(0))

    @pl.when(is_mid == 1)
    def _():
        pl.semaphore_wait(barrier, 2 * team - 1)

    send_plane(0, early_step(0), 0)
    plane_loads[1].wait()
    make_plane(0, 0)
    prod_in[0, me] = prod_out[0, me]
    send_plane(0, 0, 1)

    @pl.when(is_mid == 1)
    def _():
        pl.semaphore_wait(side_in, team)
        signal(far_side_in, peer_at(3, 0))
        signal(mids_in, peer_at(1, 0))

    plane_loads[2].wait()
    make_plane(0, early_step(2))

    @pl.when(is_outer == 1)
    def _():
        pl.semaphore_wait(mids_in, 1)

    send_plane(0, early_step(2), 0)
    plane_loads[3].wait()
    make_plane(0, early_step(3))

    pl.semaphore_wait(far_side_in, 1)

    @pl.when(is_mid == 1)
    def _():
        signal(far_side_in, peer_at(1, 0))

    send_plane(0, early_step(3), 0)
    for half in range(1, halves):
        for k in range(PLANES):
            make_plane(half, k)
        prod_in[half, me] = prod_out[half, me]

    def send_rest():
        for half in range(1, halves):
            over_peers(lambda peer, half=half: prod_copy(half, peer, me).start())
        over_peers(lambda peer: gate_copy(peer, me).start())

    off_load.wait()
    gate_load.wait()
    chosen = lax.broadcasted_iota(jnp.int32, (16, rows), 1) == off_ref[me]
    chosen = jnp.where(chosen, 1.0, 0.0).astype(jnp.bfloat16)

    def make_gate(peer):
        cols = pl.ds(pl.multiple_of(peer * group, LANES), group)
        return dot32(chosen, streams_ref[0, :, cols])[0:1, :]

    def put_gate(peer):
        gate_out[peer] = make_gate(peer)

    over_peers(put_gate)
    gate_in[me] = make_gate(me)
    pl.when(is_outer == 1)(send_rest)

    for each in tap_loads:
        each.wait()

    def segment(d, carry):
        taps_d = filter_ref[:, pl.ds(pl.multiple_of(d * BLOCK, LANES), BLOCK)]
        dims = (((1,), (1,)), ((), ()))
        value = lax.dot_general(
            fwd_hi_ref[...], taps_d, dims, preferred_element_type=jnp.float32
        ) + lax.dot_general(fwd_lo_ref[...], taps_d, dims, preferred_element_type=jnp.float32)
        for half in range(halves):
            taps[half, d] = value[:, half * width : (half + 1) * width]
        return carry

    lax.fori_loop(0, n_blocks, segment, 0)
    row_id = lax.broadcasted_iota(jnp.int32, (BLOCK, width), 0)
    sign = jnp.where(row_id % 2 == 0, 1.0, -1.0)
    for half in range(halves):
        def window(step, carry, half=half):
            d = n_blocks - 1 - step
            re = taps[half, d, :BLOCK]
            im = taps[half, d, BLOCK:]
            taps[half, d, :BLOCK] = taps[half, d - 1, :BLOCK] + sign * im
            taps[half, d, BLOCK:] = taps[half, d - 1, BLOCK:] - sign * re
            return carry

        lax.fori_loop(0, n_blocks - 1, window, 0)
        re = taps[half, 0, :BLOCK]
        im = taps[half, 0, BLOCK:]
        taps[half, 0, :BLOCK] = sign * im
        taps[half, 0, BLOCK:] = -sign * re

    def pair_of_blocks(ref, half, first):
        both = [
            ref[half, pl.ds((first + k) * per_block, per_block)].reshape(BLOCK, width)
            for k in range(2)
        ]
        return jnp.concatenate(both, axis=1)

    for each in late_loads:
        each.wait()

    def pair_at(q):
        return flip(plane, far_step(q), PLANES)

    for half in range(halves):
        over_peers(lambda peer, half=half: prod_copy(half, peer, peer).wait_recv())
        if half == 0:
            pl.when(is_mid == 1)(send_rest)

        def forward(q, carry, half=half):
            x = pair_of_blocks(prod_in, half, 2 * q)
            value = dot32(fwd_hi_ref[...], x) + dot32(fwd_lo_ref[...], x)
            spec[2 * q] = value[:, :width]
            spec[2 * q + 1] = value[:, width:]
            return carry

        lax.fori_loop(0, n_blocks // 2, forward, 0)

        def mix(tile, carry, half=half):
            re_rows = pl.ds(pl.multiple_of(tile * 8, 8), 8)
            im_rows = pl.ds(pl.multiple_of(BLOCK + tile * 8, 8), 8)
            x_re = [spec[i, re_rows] for i in range(n_blocks)]
            x_im = [spec[i, im_rows] for i in range(n_blocks)]
            for i in reversed(range(n_blocks)):
                w_re = None
                for d in range(i + 1):
                    g_re, g_im = taps[half, d, re_rows], taps[half, d, im_rows]
                    a, b = x_re[i - d], x_im[i - d]
                    t_re = a * g_re - b * g_im
                    t_im = a * g_im + b * g_re
                    w_re, w_im = (t_re, t_im) if w_re is None else (w_re + t_re, w_im + t_im)
                spec[i, re_rows] = w_re
                spec[i, im_rows] = w_im
            return carry

        lax.fori_loop(0, BLOCK // 8, mix, 0)

        def send_pair(q, half=half):
            for k in reversed(range(team)):
                peer = pair_at(q) * team + flip(spot, k, team)

                @pl.when(peer != me)
                def _():
                    filt_copy(half, peer, me).start()

        def inverse(q_step, carry, half=half):
            q = pair_at(q_step)
            w = jnp.concatenate([spec[2 * q], spec[2 * q + 1]], axis=1)
            w_hi = w.astype(jnp.bfloat16)
            w_lo = (w - w_hi.astype(jnp.float32)).astype(jnp.bfloat16)
            y = dot32(inv_hi_ref[...], w_hi) + (
                dot32(inv_hi_ref[...], w_lo) + dot32(inv_lo_ref[...], w_hi)
            )
            y = y.astype(jnp.bfloat16)
            for k in range(2):
                part = y[:, k * width : (k + 1) * width].reshape(per_block, rows, width)
                filt_out[half, pl.ds((2 * q + k) * per_block, per_block)] = part

            if half < halves - 1:

                @pl.when(q_step > 0)
                def _():
                    send_pair(q_step - 1)

            return carry

        lax.fori_loop(0, n_blocks // 2, inverse, 0)
        if half < halves - 1:
            send_pair(n_blocks // 2 - 1)

    over_peers(lambda peer: gate_copy(peer, peer).wait_recv())
    variant = lax.broadcasted_iota(jnp.int32, (n, LANES), 0)
    place = jnp.zeros((n, LANES), jnp.int32)
    for j in range(n):
        place = jnp.where(variant == j, off_ref[j], place)
    place = place[:, :1]
    column = lax.broadcasted_iota(jnp.int32, (n, n * rows), 1)
    slot = lax.broadcasted_iota(jnp.int32, (n, n * rows), 0) * rows
    pick = jnp.where(column == slot + place, 1.0, 0.0).astype(jnp.bfloat16)
    picked = [dot32(pick, filt_out[half].reshape(n * rows, width)) for half in range(halves)]
    picked = jnp.concatenate(picked, axis=1)
    gate_rows = gate_in[...].reshape(n, group)
    rows16 = (gate_rows * picked).astype(jnp.bfloat16)
    gain_rows[...] = gain_ref[...].astype(jnp.float32).reshape(1, model_width)
    gain = gain_rows[:, pl.ds(pl.multiple_of(me * group, LANES), group)]
    rows32 = rows16.astype(jnp.float32)
    weighted = (rows32 * gain).astype(jnp.bfloat16)
    raw = dot32(weighted, unembed_ref[...])
    square = jnp.sum(rows32 * rows32, axis=1, keepdims=True)
    part_out[:, :, :vocab] = raw.reshape(n, 1, vocab)
    part_out[:, :, vocab:] = jnp.broadcast_to(square, (n, LANES)).reshape(n, 1, LANES)
    part_in[me] = part_out[me]
    over_peers(lambda peer: part_copy(peer, me).start())
    over_peers(lambda peer: filt_copy(halves - 1, peer, me).start())

    def score():
        over_peers(lambda peer: part_copy(peer, peer).wait_recv())
        total = jnp.sum(part_in[...], axis=0)
        scale = lax.rsqrt(total[:, vocab : vocab + 1] / model_width + norm_eps)
        logits = total[:, :vocab] * scale
        largest = jnp.max(logits, axis=1, keepdims=True)
        log_total = largest + jnp.log(jnp.sum(jnp.exp(logits - largest), axis=1, keepdims=True))
        vocab_ids = lax.broadcasted_iota(jnp.int32, (1, vocab), 1)
        ref_logit = jnp.sum(
            jnp.where(vocab_ids == ref_id_ref[0], logits, 0.0), axis=1, keepdims=True
        )
        alt_logit = jnp.sum(
            jnp.where(vocab_ids == alt_id_ref[0], logits, 0.0), axis=1, keepdims=True
        )
        lane = lax.broadcasted_iota(jnp.int32, (1, 2), 1)
        scores_ref[...] = jnp.where(lane == 0, ref_logit - log_total, alt_logit - ref_logit)

    def finish(owner, half, value):
        cols = lanes(owner, half)
        gate = streams_ref[0, :, cols].astype(jnp.float32)
        mixed_ref[:, cols] = (gate * value.astype(jnp.float32)).astype(jnp.bfloat16)

    for half in range(halves):
        if half == halves - 1:
            score()

        finish(me, half, filt_out[half, me])

        def landed(step, carry, half=half):
            peer = partner(n - step)
            filt_copy(half, peer, peer).wait_recv()
            finish(peer, half, filt_in[half, peer])
            return carry

        lax.fori_loop(1, n, landed, 0)

    def drain(peer):
        for half in range(halves):
            prod_copy(half, peer, me).wait_send()
            filt_copy(half, peer, me).wait_send()
        gate_copy(peer, me).wait_send()
        part_copy(peer, me).wait_send()

    over_peers(drain)


def fused_shards(streams, long_filter, gain, unembed, offsets, ref_ids, alt_ids):
    n = lax.axis_size("seq")
    rows, model_width = streams.shape[1:]
    group = model_width // n
    vocab = unembed.shape[1]
    halves = group // LANES
    width = LANES
    n_blocks = n * rows // BLOCK
    cfg = (n, halves, rows, width, vocab, model_width)
    tables = [jnp.asarray(t) for t in block_tables(BLOCK)]
    vmem = pl.BlockSpec(memory_space=pltpu.VMEM)
    smem = pl.BlockSpec(memory_space=pltpu.SMEM)
    hbm = pl.BlockSpec(memory_space=pltpu.HBM)
    dma = pltpu.SemaphoreType.DMA
    block_buffer = pltpu.VMEM((halves, n, rows, width), jnp.bfloat16)
    operands = [offsets, ref_ids, alt_ids, streams, long_filter, gain, unembed] + tables
    held = [pltpu.SMEM(each.shape, each.dtype) for each in operands[:1]]
    held += [pltpu.VMEM(each.shape, each.dtype) for each in operands[3:]]
    held_out = [pltpu.with_memory_space_constraint(each, pltpu.HBM) for each in operands]
    held_out[1:3] = [ref_ids, alt_ids]
    mixed, scores = pl.pallas_call(
        functools.partial(layer_kernel, cfg),
        out_shape=(
            jax.ShapeDtypeStruct((rows, model_width), jnp.bfloat16),
            jax.ShapeDtypeStruct((1, 2), jnp.float32),
        ),
        in_specs=[hbm] + [smem] * 2 + [hbm] * (len(operands) - 3),
        out_specs=(vmem, vmem),
        scratch_shapes=held
        + [block_buffer] * 4
        + [
            pltpu.VMEM((n_blocks, 2 * BLOCK, width), jnp.float32),
            pltpu.VMEM((halves, n_blocks, 2 * BLOCK, width), jnp.float32),
            pltpu.VMEM((n, 1, group), jnp.float32),
            pltpu.VMEM((n, 1, group), jnp.float32),
            pltpu.VMEM((n, 1, vocab + LANES), jnp.float32),
            pltpu.VMEM((n, 1, vocab + LANES), jnp.float32),
            pltpu.VMEM((1, model_width), jnp.float32),
        ]
        + [dma((halves, n))] * 4
        + [dma((n,))] * 4
        + [dma((13,))]
        + [pltpu.SemaphoreType.REGULAR] * 3,
        compiler_params=pltpu.CompilerParams(
            collective_id=0, has_side_effects=True, vmem_limit_bytes=48 * 2**20
        ),
    )(*held_out)
    return (mixed, scores.T)


def shards(streams, long_filter, gain, unembed, offsets, ref_ids, alt_ids):
    n = lax.axis_size("seq")
    rows, model_width = streams.shape[1:]
    fits = (
        model_width % (n * LANES) == 0
        and BLOCK % rows == 0
        and rows % 16 == 0
        and n * rows == 2 * PLANES * BLOCK
        and n % 16 == 0
        and n & (n - 1) == 0
        and model_width // n <= 4 * LANES
        and unembed.shape[1] % LANES == 0
        and ref_ids.shape[0] == 1
        and offsets.shape[0] == n
    )
    body = fused_shards if fits else plain_shards
    return body(streams, long_filter, gain, unembed, offsets, ref_ids, alt_ids)


def solution(mesh):
    placed = (
        P(None, ("grp", "seq"), None),
        P("seq", None),
        P(),
        P("seq", None),
        P("grp"),
        P(("grp", "seq")),
        P(("grp", "seq")),
    )
    return jax.shard_map(
        shards,
        mesh=mesh,
        in_specs=placed,
        out_specs=(P(("grp", "seq"), None), P(None, ("grp", "seq"))),
        check_vma=False,
    )
```

```python
import functools
import math

import jax
import jax.numpy as jnp
import numpy as np
from jax import lax
from jax.experimental import pallas as pl
from jax.experimental.pallas import tpu as pltpu
from jax.sharding import PartitionSpec as P

norm_eps = 1e-06
highest = lax.Precision.HIGHEST
LANES = 128
BLOCK = 256
PLANES = 4
STORES = 4
GATE = jnp.bfloat16
MESH = pl.DeviceIdType.MESH


def angle_pair(left_count, right_count, period):
    product = (
        jnp.arange(left_count, dtype=jnp.int32)[:, None]
        * jnp.arange(right_count, dtype=jnp.int32)[None, :]
        % period
    )
    theta = product.astype(jnp.float32) * (2.0 * math.pi / period)
    return (jnp.cos(theta), jnp.sin(theta))


def forward_spectrum(signal, outer_cos, outer_sin, twist_cos, twist_sin, inner_cos, inner_sin):
    first_re = jnp.einsum("kn,cnm->ckm", outer_cos, signal, precision=highest)
    first_im = -jnp.einsum("kn,cnm->ckm", outer_sin, signal, precision=highest)
    middle_re = first_re * twist_cos + first_im * twist_sin
    middle_im = first_im * twist_cos - first_re * twist_sin
    spec_re = jnp.einsum("ckn,nm->ckm", middle_re, inner_cos, precision=highest) + jnp.einsum(
        "ckn,nm->ckm", middle_im, inner_sin, precision=highest
    )
    spec_im = jnp.einsum("ckn,nm->ckm", middle_im, inner_cos, precision=highest) - jnp.einsum(
        "ckn,nm->ckm", middle_re, inner_sin, precision=highest
    )
    return (spec_re, spec_im)


def causal_filter(signal_rows, kernel_rows, n_blocks):
    channels, length = signal_rows.shape
    half_rows = length // n_blocks
    outer_len = 2 * half_rows
    period = 2 * length
    outer_cos, outer_sin = angle_pair(outer_len, half_rows, outer_len)
    twist_cos, twist_sin = angle_pair(outer_len, n_blocks, period)
    inner_cos, inner_sin = angle_pair(n_blocks, n_blocks, n_blocks)
    tables = (outer_cos, outer_sin, twist_cos, twist_sin, inner_cos, inner_sin)
    signal_re, signal_im = forward_spectrum(
        signal_rows.astype(jnp.float32).reshape(channels, half_rows, n_blocks), *tables
    )
    kernel_re, kernel_im = forward_spectrum(
        kernel_rows.astype(jnp.float32).reshape(channels, half_rows, n_blocks), *tables
    )
    joint_re = signal_re * kernel_re - signal_im * kernel_im
    joint_im = signal_re * kernel_im + signal_im * kernel_re
    back_re = jnp.einsum("ckn,nm->ckm", joint_re, inner_cos, precision=highest) - jnp.einsum(
        "ckn,nm->ckm", joint_im, inner_sin, precision=highest
    )
    back_im = jnp.einsum("ckn,nm->ckm", joint_im, inner_cos, precision=highest) + jnp.einsum(
        "ckn,nm->ckm", joint_re, inner_sin, precision=highest
    )
    turned_re = back_re * twist_cos - back_im * twist_sin
    turned_im = back_im * twist_cos + back_re * twist_sin
    result = jnp.einsum("kn,ckm->cnm", outer_cos, turned_re, precision=highest) - jnp.einsum(
        "kn,ckm->cnm", outer_sin, turned_im, precision=highest
    )
    return (result / period).reshape(channels, length)


def variant_scores(raw_terms, square_terms, model_width, ref_ids, alt_ids):
    logits = raw_terms * lax.rsqrt(square_terms / model_width + norm_eps)[:, None]
    largest = jnp.max(logits, axis=1)
    log_total = largest + jnp.log(jnp.sum(jnp.exp(logits - largest[:, None]), axis=1))
    vocab_ids = jnp.arange(logits.shape[1], dtype=jnp.int32)
    ref_logit = jnp.sum(jnp.where(vocab_ids[None, :] == ref_ids[:, None], logits, 0.0), axis=1)
    alt_logit = jnp.sum(jnp.where(vocab_ids[None, :] == alt_ids[:, None], logits, 0.0), axis=1)
    return jnp.stack([ref_logit - log_total, alt_logit - ref_logit])


def pick_local(mixed, offsets, my_index, vars_dev):
    stride_rows = mixed.shape[0] // vars_dev
    local_offsets = lax.dynamic_slice_in_dim(offsets, my_index * vars_dev, vars_dev)
    row_index = jnp.arange(vars_dev, dtype=jnp.int32) * stride_rows + local_offsets
    return mixed[row_index]


def plain_shards(streams, long_filter, gain, unembed, offsets, ref_ids, alt_ids):
    n_devices = lax.axis_size("seq")
    my_index = lax.axis_index("seq")
    tok_rows = streams.shape[1]
    model_width = streams.shape[2]
    group_width = model_width // n_devices
    length = tok_rows * n_devices
    vars_dev = ref_ids.shape[0]
    products = (streams[1].astype(jnp.float32) * streams[2].astype(jnp.float32)).astype(
        jnp.bfloat16
    )
    split_view = products.reshape(tok_rows, n_devices, group_width)
    moved_prod = lax.all_to_all(split_view, "seq", split_axis=1, concat_axis=0, tiled=True)
    convolved = causal_filter(moved_prod.reshape(length, group_width).T, long_filter, n_devices)
    filtered_back = convolved.astype(jnp.bfloat16).T.reshape(length, 1, group_width)
    filtered = lax.all_to_all(
        filtered_back, "seq", split_axis=0, concat_axis=1, tiled=True
    ).reshape(tok_rows, model_width)
    mixed = (streams[0].astype(jnp.float32) * filtered.astype(jnp.float32)).astype(jnp.bfloat16)
    picked = pick_local(mixed, offsets, my_index, vars_dev)
    weighted = (picked.astype(jnp.float32) * gain.astype(jnp.float32)[None, :]).astype(jnp.bfloat16)
    square_terms = jnp.sum(jnp.square(picked.astype(jnp.float32)), axis=1)
    raw_terms = jnp.dot(
        weighted,
        lax.all_gather(unembed, "seq", axis=0, tiled=True),
        preferred_element_type=jnp.float32,
    )
    scores = variant_scores(raw_terms, square_terms, model_width, ref_ids, alt_ids)
    return (mixed, scores)


def block_tables(block):
    freq = 2 * np.arange(block)[:, None] + 1
    time = np.arange(block)[None, :]
    period = 4 * block
    theta = (freq * time % period) * (2.0 * np.pi / period)
    forward = np.concatenate([np.cos(theta), -np.sin(theta)], axis=0)
    theta = (freq * (time + block) % period).T * (2.0 * np.pi / period)
    inverse = np.concatenate([np.cos(theta), -np.sin(theta)], axis=1) / block
    split = []
    for table in (forward, inverse):
        high = table.astype(np.float32).astype(jnp.bfloat16)
        low = (table - high.astype(np.float64)).astype(np.float32).astype(jnp.bfloat16)
        split += [high, low]
    return split


def dot32(left, right):
    return jnp.dot(left, right, preferred_element_type=jnp.float32)


def layer_kernel(
    cfg,
    off_hbm, ref_id_ref, alt_id_ref,
    streams_hbm, filter_hbm, gain_hbm, unembed_hbm,
    fwd_hi_hbm, fwd_lo_hbm, inv_hi_hbm, inv_lo_hbm,
    mixed_ref, scores_ref,
    off_ref,
    streams_ref, filter_ref, gain_ref, unembed_ref,
    fwd_hi_ref, fwd_lo_ref, inv_hi_ref, inv_lo_ref,
    prod_out, prod_in, filt_out, filt_in, spec, taps,
    gate_out, gate_in, part_out, part_in, line_out, line_in, gain_rows,
    ps_sem, pr_sem, fs_sem, fr_sem, gs_sem, gr_sem, qs_sem, qr_sem, ls_sem, lr_sem, in_sem,
    side_in, mids_in, far_side_in,
):
    n, halves, rows, width, vocab, model_width = cfg
    me = lax.axis_index("seq")
    n_blocks = n * rows // BLOCK
    per_block = BLOCK // rows
    group = halves * width

    barrier = pltpu.get_barrier_semaphore()

    team = n // PLANES
    plane = me // team
    spot = lax.rem(me, team)
    is_mid = lax.rem((plane + 1) // 2, 2)
    is_outer = 1 - is_mid

    def flip(value, step, size):
        bit, out = 1, 0
        while bit < size:
            out = out + bit * lax.rem(value // bit + step // bit, 2)
            bit *= 2
        return out

    def peer_at(plane_step, spot_step):
        return flip(plane, plane_step, PLANES) * team + flip(spot, spot_step, team)

    def far_step(k):
        return 3 - k + jnp.where(k < 2, is_mid * (2 * k - 1), 0)

    def partner(k):
        return peer_at(far_step((k - 1) // team), team - 1 - lax.rem(k - 1, team))

    def rank(owner):
        return lax.rem(owner, team) * PLANES + owner // team

    def signal(sem, peer):
        pl.semaphore_signal(sem, inc=1, device_id={"seq": peer}, device_id_type=MESH)

    def greet(plane_step, first):
        for k in range(first, team):
            signal(barrier, peer_at(plane_step, k))

    @pl.when(is_mid == 1)
    def _():
        greet(3, 0)
        greet(1, 0)

    greet(0, 1)

    def early_step(k):
        mid_steps, outer_steps = (3, 0, 1, 2), (1, 0, 2, 3)
        return outer_steps[k] + (mid_steps[k] - outer_steps[k]) * is_mid

    def plane_stream(k):
        share = model_width // PLANES
        first = pl.multiple_of(flip(plane, early_step(k), PLANES) * share, LANES)
        part = (pl.ds(1, 2), slice(None), pl.ds(first, share))
        return pltpu.make_async_copy(streams_hbm.at[part], streams_ref.at[part], in_sem.at[k])

    def load(src, dst, sem):
        return pltpu.make_async_copy(src, dst, in_sem.at[sem])

    plane_loads = [plane_stream(k) for k in range(PLANES)]
    gate_load = load(streams_hbm.at[0], streams_ref.at[0], 4)
    off_load = load(off_hbm, off_ref, 5)
    tap_loads = [
        load(filter_hbm, filter_ref, 6),
        load(fwd_hi_hbm, fwd_hi_ref, 7),
        load(fwd_lo_hbm, fwd_lo_ref, 8),
    ]
    late_loads = [
        load(inv_hi_hbm, inv_hi_ref, 9),
        load(inv_lo_hbm, inv_lo_ref, 10),
        load(gain_hbm, gain_ref, 11),
        load(unembed_hbm, unembed_ref, 12),
    ]
    for each in plane_loads + [off_load, gate_load] + tap_loads + late_loads:
        each.start()

    def lanes(owner, half):
        return pl.ds(pl.multiple_of(owner * group + half * width, LANES), width)

    def product(owner, half):
        cols = lanes(owner, half)
        left = streams_ref[1, :, cols].astype(jnp.float32)
        right = streams_ref[2, :, cols].astype(jnp.float32)
        return (left * right).astype(jnp.bfloat16)

    def copy(src, dst, send_sem, recv_sem, peer):
        return pltpu.make_async_remote_copy(
            src_ref=src, dst_ref=dst, send_sem=send_sem, recv_sem=recv_sem,
            device_id={"seq": peer}, device_id_type=MESH,
        )

    def prod_copy(half, peer, slot):
        return copy(
            prod_out.at[half, peer], prod_in.at[half, slot],
            ps_sem.at[half, peer], pr_sem.at[half, slot], peer,
        )

    def filt_copy(half, peer, slot):
        return copy(
            filt_out.at[half, peer], filt_in.at[half, slot],
            fs_sem.at[half, peer], fr_sem.at[half, slot], peer,
        )

    def gate_copy(peer, slot):
        return copy(
            gate_out.at[peer], gate_in.at[rank(slot)], gs_sem.at[peer], gr_sem.at[slot], peer
        )

    def part_copy(step, slot):
        mate = flip(spot, step, team)
        return copy(
            part_out.at[mate], part_in.at[slot], qs_sem.at[mate], qr_sem.at[slot],
            peer_at(0, step),
        )

    def line_copy(step, slot):
        other = flip(plane, step, PLANES)
        return copy(
            line_out.at[other], line_in.at[slot], ls_sem.at[other], lr_sem.at[slot],
            peer_at(step, 0),
        )

    def over_peers(body):
        def step(k, carry):
            body(partner(k))
            return carry

        lax.fori_loop(1, n, step, 0)

    def make_plane(half, plane_step):
        def step(k, carry):
            owner = peer_at(plane_step, k)
            prod_out[half, owner] = product(owner, half)
            return carry

        lax.fori_loop(0, team, step, 0)

    def send_plane(half, plane_step, first):
        def step(k, carry):
            prod_copy(half, peer_at(plane_step, k), me).start()
            return carry

        lax.fori_loop(first, team, step, 0)

    @pl.when(is_outer == 1)
    def _():
        pl.semaphore_wait(barrier, 2 * team - 1)
        for k in range(team):
            signal(side_in, peer_at(1, k))

    plane_loads[0].wait()
    make_plane(0, early_step(0))

    @pl.when(is_mid == 1)
    def _():
        pl.semaphore_wait(barrier, 2 * team - 1)

    send_plane(0, early_step(0), 0)
    plane_loads[1].wait()
    make_plane(0, 0)
    prod_in[0, me] = prod_out[0, me]
    send_plane(0, 0, 1)

    @pl.when(is_mid == 1)
    def _():
        pl.semaphore_wait(side_in, team)
        signal(far_side_in, peer_at(3, 0))
        signal(mids_in, peer_at(1, 0))

    plane_loads[2].wait()
    make_plane(0, early_step(2))

    @pl.when(is_outer == 1)
    def _():
        pl.semaphore_wait(mids_in, 1)

    send_plane(0, early_step(2), 0)
    plane_loads[3].wait()
    make_plane(0, early_step(3))

    pl.semaphore_wait(far_side_in, 1)

    @pl.when(is_mid == 1)
    def _():
        signal(far_side_in, peer_at(1, 0))

    send_plane(0, early_step(3), 0)
    for half in range(1, halves):
        for k in range(PLANES):
            make_plane(half, k)
        prod_in[half, me] = prod_out[half, me]

    def send_rest():
        for half in range(1, halves):
            over_peers(lambda peer, half=half: prod_copy(half, peer, me).start())
        over_peers(lambda peer: gate_copy(peer, me).start())

    off_load.wait()
    gate_load.wait()
    chosen = lax.broadcasted_iota(jnp.int32, (16, rows), 1) == off_ref[me]
    chosen = jnp.where(chosen, 1.0, 0.0).astype(jnp.bfloat16)

    def make_gate(peer):
        cols = pl.ds(pl.multiple_of(peer * group, LANES), group)
        return dot32(chosen, streams_ref[0, :, cols])[0:1, :].astype(GATE)

    def put_gate(peer):
        gate_out[peer] = make_gate(peer)

    over_peers(put_gate)
    gate_in[rank(me)] = make_gate(me)
    pl.when(is_outer == 1)(send_rest)

    for each in tap_loads:
        each.wait()

    def segment(d, carry):
        taps_d = filter_ref[:, pl.ds(pl.multiple_of(d * BLOCK, LANES), BLOCK)]
        dims = (((1,), (1,)), ((), ()))
        value = lax.dot_general(
            fwd_hi_ref[...], taps_d, dims, preferred_element_type=jnp.float32
        ) + lax.dot_general(fwd_lo_ref[...], taps_d, dims, preferred_element_type=jnp.float32)
        for half in range(halves):
            taps[half, d] = value[:, half * width : (half + 1) * width]
        return carry

    lax.fori_loop(0, n_blocks, segment, 0)
    row_id = lax.broadcasted_iota(jnp.int32, (BLOCK, width), 0)
    sign = jnp.where(row_id % 2 == 0, 1.0, -1.0)
    for half in range(halves):
        def window(step, carry, half=half):
            d = n_blocks - 1 - step
            re = taps[half, d, :BLOCK]
            im = taps[half, d, BLOCK:]
            taps[half, d, :BLOCK] = taps[half, d - 1, :BLOCK] + sign * im
            taps[half, d, BLOCK:] = taps[half, d - 1, BLOCK:] - sign * re
            return carry

        lax.fori_loop(0, n_blocks - 1, window, 0)
        re = taps[half, 0, :BLOCK]
        im = taps[half, 0, BLOCK:]
        taps[half, 0, :BLOCK] = sign * im
        taps[half, 0, BLOCK:] = -sign * re

    def pair_of_blocks(ref, half, first):
        both = [
            ref[half, pl.ds((first + k) * per_block, per_block)].reshape(BLOCK, width)
            for k in range(2)
        ]
        return jnp.concatenate(both, axis=1)

    for each in late_loads:
        each.wait()

    def pair_at(q):
        return flip(plane, far_step(q), PLANES)

    def send_pair(q, half):
        for k in reversed(range(team)):
            peer = pair_at(q) * team + flip(spot, k, team)

            @pl.when(peer != me)
            def _():
                filt_copy(half, peer, me).start()

    for half in range(halves):
        over_peers(lambda peer, half=half: prod_copy(half, peer, peer).wait_recv())
        if half == 0:
            pl.when(is_mid == 1)(send_rest)

        def forward(q, carry, half=half):
            x = pair_of_blocks(prod_in, half, 2 * q)
            value = dot32(fwd_hi_ref[...], x) + dot32(fwd_lo_ref[...], x)
            spec[2 * q] = value[:, :width]
            spec[2 * q + 1] = value[:, width:]
            return carry

        lax.fori_loop(0, n_blocks // 2, forward, 0)

        def mix(tile, carry, half=half):
            re_rows = pl.ds(pl.multiple_of(tile * 8, 8), 8)
            im_rows = pl.ds(pl.multiple_of(BLOCK + tile * 8, 8), 8)
            x_re = [spec[i, re_rows] for i in range(n_blocks)]
            x_im = [spec[i, im_rows] for i in range(n_blocks)]
            for i in reversed(range(n_blocks)):
                w_re = None
                for d in range(i + 1):
                    g_re, g_im = taps[half, d, re_rows], taps[half, d, im_rows]
                    a, b = x_re[i - d], x_im[i - d]
                    t_re = a * g_re - b * g_im
                    t_im = a * g_im + b * g_re
                    w_re, w_im = (t_re, t_im) if w_re is None else (w_re + t_re, w_im + t_im)
                spec[i, re_rows] = w_re
                spec[i, im_rows] = w_im
            return carry

        lax.fori_loop(0, BLOCK // 8, mix, 0)

        def inverse(q_step, carry, half=half):
            q = pair_at(q_step)
            w = jnp.concatenate([spec[2 * q], spec[2 * q + 1]], axis=1)
            w_hi = w.astype(jnp.bfloat16)
            w_lo = (w - w_hi.astype(jnp.float32)).astype(jnp.bfloat16)
            y = dot32(inv_hi_ref[...], w_hi) + (
                dot32(inv_hi_ref[...], w_lo) + dot32(inv_lo_ref[...], w_hi)
            )
            y = y.astype(jnp.bfloat16)
            for k in range(2):
                part = y[:, k * width : (k + 1) * width].reshape(per_block, rows, width)
                filt_out[half, pl.ds((2 * q + k) * per_block, per_block)] = part

            @pl.when(q_step > 0 if half < halves - 1 else q_step == 1)
            def _():
                send_pair(q_step - 1, half)

            return carry

        lax.fori_loop(0, n_blocks // 2, inverse, 0)
        if half < halves - 1:
            send_pair(n_blocks // 2 - 1, half)

    def finish(owner, half, value):
        cols = lanes(owner, half)
        gate = streams_ref[0, :, cols].astype(jnp.float32)
        mixed_ref[:, cols] = (gate * value.astype(jnp.float32)).astype(jnp.bfloat16)

    over_peers(lambda peer: gate_copy(peer, peer).wait_recv())
    variant = lax.broadcasted_iota(jnp.int32, (n, LANES), 0)
    place = jnp.zeros((n, LANES), jnp.int32)
    for j in range(n):
        j_rank = j % team * PLANES + j // team
        place = jnp.where(variant == j_rank, off_ref[j] + j * rows, place)
    column = lax.broadcasted_iota(jnp.int32, (n, n * rows), 1)
    pick = jnp.where(column == place[:, :1], 1.0, 0.0).astype(jnp.bfloat16)
    picked = [dot32(pick, filt_out[half].reshape(n * rows, width)) for half in range(halves)]
    picked = jnp.concatenate(picked, axis=1)
    gate_rows = gate_in[...].astype(jnp.float32).reshape(n, group)
    rows16 = (gate_rows * picked).astype(jnp.bfloat16)
    gain_rows[...] = gain_ref[...].astype(jnp.float32).reshape(1, model_width)
    gain = gain_rows[:, pl.ds(pl.multiple_of(me * group, LANES), group)]
    rows32 = rows16.astype(jnp.float32)
    weighted = (rows32 * gain).astype(jnp.bfloat16)
    raw = dot32(weighted, unembed_ref[...])
    square = jnp.sum(rows32 * rows32, axis=1, keepdims=True)
    part_out[:, :, :vocab] = raw.reshape(team, PLANES, vocab)
    part_out[:, :, vocab:] = jnp.broadcast_to(square, (n, LANES)).reshape(team, PLANES, LANES)
    part_in[spot] = part_out[spot]
    for k in range(1, team):
        part_copy(k, spot).start()
    for half in range(halves):
        finish(me, half, filt_out[half, me])
    for k in range(1, team):
        part_copy(k, flip(spot, k, team)).wait_recv()
    line_out[...] = jnp.sum(part_in[...], axis=0).reshape(PLANES, 1, vocab + LANES)
    line_in[plane] = line_out[plane]
    for k in reversed(range(1, PLANES)):
        line_copy(k, plane).start()
    for k in range(1, n_blocks // 2):
        send_pair(k, halves - 1)

    def score():
        for k in range(1, PLANES):
            line_copy(k, flip(plane, k, PLANES)).wait_recv()
        total = jnp.sum(line_in[...], axis=0)
        scale = lax.rsqrt(total[:, vocab : vocab + 1] / model_width + norm_eps)
        logits = total[:, :vocab] * scale
        largest = jnp.max(logits, axis=1, keepdims=True)
        log_total = largest + jnp.log(jnp.sum(jnp.exp(logits - largest), axis=1, keepdims=True))
        vocab_ids = lax.broadcasted_iota(jnp.int32, (1, vocab), 1)
        ref_logit = jnp.sum(
            jnp.where(vocab_ids == ref_id_ref[0], logits, 0.0), axis=1, keepdims=True
        )
        alt_logit = jnp.sum(
            jnp.where(vocab_ids == alt_id_ref[0], logits, 0.0), axis=1, keepdims=True
        )
        lane = lax.broadcasted_iota(jnp.int32, (1, 2), 1)
        scores_ref[...] = jnp.where(lane == 0, ref_logit - log_total, alt_logit - ref_logit)

    for half in range(halves):
        if half == halves - 1:
            score()

        def landed(step, carry, half=half):
            peer = partner(n - step)
            filt_copy(half, peer, peer).wait_recv()
            finish(peer, half, filt_in[half, peer])
            return carry

        lax.fori_loop(1, n, landed, 0)

    def drain(peer):
        for half in range(halves):
            prod_copy(half, peer, me).wait_send()
            filt_copy(half, peer, me).wait_send()
        gate_copy(peer, me).wait_send()

    over_peers(drain)
    for k in range(1, team):
        part_copy(k, spot).wait_send()
    for k in range(1, PLANES):
        line_copy(k, plane).wait_send()


def store_kernel(mixed_ref, scores_ref, mixed_hbm, scores_hbm, sem):
    share = mixed_ref.shape[0] // STORES
    moves = [pltpu.make_async_copy(scores_ref, scores_hbm, sem.at[STORES])]
    for k in range(STORES):
        part = pl.ds(k * share, share)
        moves.append(pltpu.make_async_copy(mixed_ref.at[part], mixed_hbm.at[part], sem.at[k]))
    for move in moves:
        move.start()
    for move in moves:
        move.wait()


def fused_shards(streams, long_filter, gain, unembed, offsets, ref_ids, alt_ids):
    n = lax.axis_size("seq")
    rows, model_width = streams.shape[1:]
    group = model_width // n
    team = n // PLANES
    vocab = unembed.shape[1]
    halves = group // LANES
    width = LANES
    n_blocks = n * rows // BLOCK
    cfg = (n, halves, rows, width, vocab, model_width)
    tables = [jnp.asarray(t) for t in block_tables(BLOCK)]
    vmem = pl.BlockSpec(memory_space=pltpu.VMEM)
    smem = pl.BlockSpec(memory_space=pltpu.SMEM)
    hbm = pl.BlockSpec(memory_space=pltpu.HBM)
    dma = pltpu.SemaphoreType.DMA
    block_buffer = pltpu.VMEM((halves, n, rows, width), jnp.bfloat16)
    operands = [offsets, ref_ids, alt_ids, streams, long_filter, gain, unembed] + tables
    held = [pltpu.SMEM(each.shape, each.dtype) for each in operands[:1]]
    held += [pltpu.VMEM(each.shape, each.dtype) for each in operands[3:]]
    held_out = [pltpu.with_memory_space_constraint(each, pltpu.HBM) for each in operands]
    held_out[1:3] = [ref_ids, alt_ids]
    mixed, scores = pl.pallas_call(
        functools.partial(layer_kernel, cfg),
        out_shape=(
            jax.ShapeDtypeStruct((rows, model_width), jnp.bfloat16),
            jax.ShapeDtypeStruct((1, 2), jnp.float32),
        ),
        in_specs=[hbm] + [smem] * 2 + [hbm] * (len(operands) - 3),
        out_specs=(vmem, vmem),
        scratch_shapes=held
        + [block_buffer] * 4
        + [
            pltpu.VMEM((n_blocks, 2 * BLOCK, width), jnp.float32),
            pltpu.VMEM((halves, n_blocks, 2 * BLOCK, width), jnp.float32),
            pltpu.VMEM((n, 1, group), GATE),
            pltpu.VMEM((n, 1, group), GATE),
            pltpu.VMEM((team, PLANES, vocab + LANES), jnp.float32),
            pltpu.VMEM((team, PLANES, vocab + LANES), jnp.float32),
            pltpu.VMEM((PLANES, 1, vocab + LANES), jnp.float32),
            pltpu.VMEM((PLANES, 1, vocab + LANES), jnp.float32),
            pltpu.VMEM((1, model_width), jnp.float32),
        ]
        + [dma((halves, n))] * 4
        + [dma((n,))] * 2
        + [dma((team,))] * 2
        + [dma((PLANES,))] * 2
        + [dma((13,))]
        + [pltpu.SemaphoreType.REGULAR] * 3,
        compiler_params=pltpu.CompilerParams(
            collective_id=0, has_side_effects=True, vmem_limit_bytes=48 * 2**20
        ),
    )(*held_out)
    mixed, scores = pl.pallas_call(
        store_kernel,
        out_shape=(
            jax.ShapeDtypeStruct(mixed.shape, mixed.dtype),
            jax.ShapeDtypeStruct(scores.shape, scores.dtype),
        ),
        in_specs=[vmem, vmem],
        out_specs=(hbm, hbm),
        scratch_shapes=[dma((STORES + 1,))],
    )(
        pltpu.with_memory_space_constraint(mixed, pltpu.VMEM),
        pltpu.with_memory_space_constraint(scores, pltpu.VMEM),
    )
    return (mixed, scores.T)


def shards(streams, long_filter, gain, unembed, offsets, ref_ids, alt_ids):
    n = lax.axis_size("seq")
    rows, model_width = streams.shape[1:]
    fits = (
        model_width % (n * LANES) == 0
        and BLOCK % rows == 0
        and rows % 16 == 0
        and n * rows == 2 * PLANES * BLOCK
        and n % 16 == 0
        and n & (n - 1) == 0
        and model_width // n <= 4 * LANES
        and unembed.shape[1] % LANES == 0
        and ref_ids.shape[0] == 1
        and offsets.shape[0] == n
    )
    body = fused_shards if fits else plain_shards
    return body(streams, long_filter, gain, unembed, offsets, ref_ids, alt_ids)


def solution(mesh):
    placed = (
        P(None, ("grp", "seq"), None),
        P("seq", None),
        P(),
        P("seq", None),
        P("grp"),
        P(("grp", "seq")),
        P(("grp", "seq")),
    )
    return jax.shard_map(
        shards,
        mesh=mesh,
        in_specs=placed,
        out_specs=(P(("grp", "seq"), None), P(None, ("grp", "seq"))),
        check_vma=False,
    )
```

```python
import functools
import math

import jax
import jax.numpy as jnp
import numpy as np
from jax import lax
from jax.experimental import pallas as pl
from jax.experimental.pallas import tpu as pltpu
from jax.sharding import PartitionSpec as P

norm_eps = 1e-06
highest = lax.Precision.HIGHEST
LANES = 128
BLOCK = 256
PLANES = 4
STORES = 4
GATE = jnp.bfloat16
MESH = pl.DeviceIdType.MESH


def angle_pair(left_count, right_count, period):
    product = (
        jnp.arange(left_count, dtype=jnp.int32)[:, None]
        * jnp.arange(right_count, dtype=jnp.int32)[None, :]
        % period
    )
    theta = product.astype(jnp.float32) * (2.0 * math.pi / period)
    return (jnp.cos(theta), jnp.sin(theta))


def forward_spectrum(signal, outer_cos, outer_sin, twist_cos, twist_sin, inner_cos, inner_sin):
    first_re = jnp.einsum("kn,cnm->ckm", outer_cos, signal, precision=highest)
    first_im = -jnp.einsum("kn,cnm->ckm", outer_sin, signal, precision=highest)
    middle_re = first_re * twist_cos + first_im * twist_sin
    middle_im = first_im * twist_cos - first_re * twist_sin
    spec_re = jnp.einsum("ckn,nm->ckm", middle_re, inner_cos, precision=highest) + jnp.einsum(
        "ckn,nm->ckm", middle_im, inner_sin, precision=highest
    )
    spec_im = jnp.einsum("ckn,nm->ckm", middle_im, inner_cos, precision=highest) - jnp.einsum(
        "ckn,nm->ckm", middle_re, inner_sin, precision=highest
    )
    return (spec_re, spec_im)


def causal_filter(signal_rows, kernel_rows, n_blocks):
    channels, length = signal_rows.shape
    half_rows = length // n_blocks
    outer_len = 2 * half_rows
    period = 2 * length
    outer_cos, outer_sin = angle_pair(outer_len, half_rows, outer_len)
    twist_cos, twist_sin = angle_pair(outer_len, n_blocks, period)
    inner_cos, inner_sin = angle_pair(n_blocks, n_blocks, n_blocks)
    tables = (outer_cos, outer_sin, twist_cos, twist_sin, inner_cos, inner_sin)
    signal_re, signal_im = forward_spectrum(
        signal_rows.astype(jnp.float32).reshape(channels, half_rows, n_blocks), *tables
    )
    kernel_re, kernel_im = forward_spectrum(
        kernel_rows.astype(jnp.float32).reshape(channels, half_rows, n_blocks), *tables
    )
    joint_re = signal_re * kernel_re - signal_im * kernel_im
    joint_im = signal_re * kernel_im + signal_im * kernel_re
    back_re = jnp.einsum("ckn,nm->ckm", joint_re, inner_cos, precision=highest) - jnp.einsum(
        "ckn,nm->ckm", joint_im, inner_sin, precision=highest
    )
    back_im = jnp.einsum("ckn,nm->ckm", joint_im, inner_cos, precision=highest) + jnp.einsum(
        "ckn,nm->ckm", joint_re, inner_sin, precision=highest
    )
    turned_re = back_re * twist_cos - back_im * twist_sin
    turned_im = back_im * twist_cos + back_re * twist_sin
    result = jnp.einsum("kn,ckm->cnm", outer_cos, turned_re, precision=highest) - jnp.einsum(
        "kn,ckm->cnm", outer_sin, turned_im, precision=highest
    )
    return (result / period).reshape(channels, length)


def variant_scores(raw_terms, square_terms, model_width, ref_ids, alt_ids):
    logits = raw_terms * lax.rsqrt(square_terms / model_width + norm_eps)[:, None]
    largest = jnp.max(logits, axis=1)
    log_total = largest + jnp.log(jnp.sum(jnp.exp(logits - largest[:, None]), axis=1))
    vocab_ids = jnp.arange(logits.shape[1], dtype=jnp.int32)
    ref_logit = jnp.sum(jnp.where(vocab_ids[None, :] == ref_ids[:, None], logits, 0.0), axis=1)
    alt_logit = jnp.sum(jnp.where(vocab_ids[None, :] == alt_ids[:, None], logits, 0.0), axis=1)
    return jnp.stack([ref_logit - log_total, alt_logit - ref_logit])


def pick_local(mixed, offsets, my_index, vars_dev):
    stride_rows = mixed.shape[0] // vars_dev
    local_offsets = lax.dynamic_slice_in_dim(offsets, my_index * vars_dev, vars_dev)
    row_index = jnp.arange(vars_dev, dtype=jnp.int32) * stride_rows + local_offsets
    return mixed[row_index]


def plain_shards(streams, long_filter, gain, unembed, offsets, ref_ids, alt_ids):
    n_devices = lax.axis_size("seq")
    my_index = lax.axis_index("seq")
    tok_rows = streams.shape[1]
    model_width = streams.shape[2]
    group_width = model_width // n_devices
    length = tok_rows * n_devices
    vars_dev = ref_ids.shape[0]
    products = (streams[1].astype(jnp.float32) * streams[2].astype(jnp.float32)).astype(
        jnp.bfloat16
    )
    split_view = products.reshape(tok_rows, n_devices, group_width)
    moved_prod = lax.all_to_all(split_view, "seq", split_axis=1, concat_axis=0, tiled=True)
    convolved = causal_filter(moved_prod.reshape(length, group_width).T, long_filter, n_devices)
    filtered_back = convolved.astype(jnp.bfloat16).T.reshape(length, 1, group_width)
    filtered = lax.all_to_all(
        filtered_back, "seq", split_axis=0, concat_axis=1, tiled=True
    ).reshape(tok_rows, model_width)
    mixed = (streams[0].astype(jnp.float32) * filtered.astype(jnp.float32)).astype(jnp.bfloat16)
    picked = pick_local(mixed, offsets, my_index, vars_dev)
    weighted = (picked.astype(jnp.float32) * gain.astype(jnp.float32)[None, :]).astype(jnp.bfloat16)
    square_terms = jnp.sum(jnp.square(picked.astype(jnp.float32)), axis=1)
    raw_terms = jnp.dot(
        weighted,
        lax.all_gather(unembed, "seq", axis=0, tiled=True),
        preferred_element_type=jnp.float32,
    )
    scores = variant_scores(raw_terms, square_terms, model_width, ref_ids, alt_ids)
    return (mixed, scores)


def block_tables(block):
    freq = 2 * np.arange(block)[:, None] + 1
    time = np.arange(block)[None, :]
    period = 4 * block
    theta = (freq * time % period) * (2.0 * np.pi / period)
    forward = np.concatenate([np.cos(theta), -np.sin(theta)], axis=0)
    theta = (freq * (time + block) % period).T * (2.0 * np.pi / period)
    inverse = np.concatenate([np.cos(theta), -np.sin(theta)], axis=1) / block
    split = []
    for table in (forward, inverse):
        high = table.astype(np.float32).astype(jnp.bfloat16)
        low = (table - high.astype(np.float64)).astype(np.float32).astype(jnp.bfloat16)
        split += [high, low]
    return split


def dot32(left, right):
    return jnp.dot(left, right, preferred_element_type=jnp.float32)


def layer_kernel(
    cfg,
    off_hbm, ref_id_ref, alt_id_ref,
    streams_hbm, filter_hbm, gain_hbm, unembed_hbm,
    fwd_hi_hbm, fwd_lo_hbm, inv_hi_hbm, inv_lo_hbm,
    mixed_ref, scores_ref,
    off_ref,
    streams_ref, filter_ref, gain_ref, unembed_ref,
    fwd_hi_ref, fwd_lo_ref, inv_hi_ref, inv_lo_ref,
    prod_out, prod_in, filt_out, filt_in, spec, taps,
    gate_out, gate_mid, gate_in, part_out, part_in, line_out, line_in, gain_rows,
    ps_sem, pr_sem, fs_sem, fr_sem, gs_sem, gr_sem, hs_sem, hr_sem, qs_sem, qr_sem, ls_sem, lr_sem, in_sem,
    side_in, mids_in, far_side_in,
):
    n, halves, rows, width, vocab, model_width = cfg
    me = lax.axis_index("seq")
    n_blocks = n * rows // BLOCK
    per_block = BLOCK // rows
    group = halves * width

    barrier = pltpu.get_barrier_semaphore()

    team = n // PLANES
    plane = me // team
    spot = lax.rem(me, team)
    is_mid = lax.rem((plane + 1) // 2, 2)
    is_outer = 1 - is_mid

    def flip(value, step, size):
        bit, out = 1, 0
        while bit < size:
            out = out + bit * lax.rem(value // bit + step // bit, 2)
            bit *= 2
        return out

    def peer_at(plane_step, spot_step):
        return flip(plane, plane_step, PLANES) * team + flip(spot, spot_step, team)

    def far_step(k):
        return 3 - k + jnp.where(k < 2, is_mid * (2 * k - 1), 0)

    def partner(k):
        return peer_at(far_step((k - 1) // team), team - 1 - lax.rem(k - 1, team))

    def signal(sem, peer):
        pl.semaphore_signal(sem, inc=1, device_id={"seq": peer}, device_id_type=MESH)

    def greet(plane_step, first):
        for k in range(first, team):
            signal(barrier, peer_at(plane_step, k))

    @pl.when(is_mid == 1)
    def _():
        greet(3, 0)
        greet(1, 0)

    greet(0, 1)

    def early_step(k):
        mid_steps, outer_steps = (3, 0, 1, 2), (1, 0, 2, 3)
        return outer_steps[k] + (mid_steps[k] - outer_steps[k]) * is_mid

    def plane_stream(k):
        share = model_width // PLANES
        first = pl.multiple_of(flip(plane, early_step(k), PLANES) * share, LANES)
        part = (pl.ds(1, 2), slice(None), pl.ds(first, share))
        return pltpu.make_async_copy(streams_hbm.at[part], streams_ref.at[part], in_sem.at[k])

    def load(src, dst, sem):
        return pltpu.make_async_copy(src, dst, in_sem.at[sem])

    plane_loads = [plane_stream(k) for k in range(PLANES)]
    gate_load = load(streams_hbm.at[0], streams_ref.at[0], 4)
    off_load = load(off_hbm, off_ref, 5)
    tap_loads = [
        load(filter_hbm, filter_ref, 6),
        load(fwd_hi_hbm, fwd_hi_ref, 7),
        load(fwd_lo_hbm, fwd_lo_ref, 8),
    ]
    late_loads = [
        load(inv_hi_hbm, inv_hi_ref, 9),
        load(inv_lo_hbm, inv_lo_ref, 10),
        load(gain_hbm, gain_ref, 11),
        load(unembed_hbm, unembed_ref, 12),
    ]
    for each in plane_loads + [off_load, gate_load] + tap_loads + late_loads:
        each.start()

    def lanes(owner, half):
        return pl.ds(pl.multiple_of(owner * group + half * width, LANES), width)

    def product(owner, half):
        cols = lanes(owner, half)
        left = streams_ref[1, :, cols].astype(jnp.float32)
        right = streams_ref[2, :, cols].astype(jnp.float32)
        return (left * right).astype(jnp.bfloat16)

    def copy(src, dst, send_sem, recv_sem, peer):
        return pltpu.make_async_remote_copy(
            src_ref=src, dst_ref=dst, send_sem=send_sem, recv_sem=recv_sem,
            device_id={"seq": peer}, device_id_type=MESH,
        )

    def prod_copy(half, peer, slot):
        return copy(
            prod_out.at[half, peer], prod_in.at[half, slot],
            ps_sem.at[half, peer], pr_sem.at[half, slot], peer,
        )

    def filt_copy(half, peer, slot):
        return copy(
            filt_out.at[half, peer], filt_in.at[half, slot],
            fs_sem.at[half, peer], fr_sem.at[half, slot], peer,
        )

    def gate_line(step, slot):
        other = flip(plane, step, PLANES)
        return copy(
            gate_out.at[pl.ds(other * team, team)], gate_mid.at[slot],
            gs_sem.at[other], gr_sem.at[slot], peer_at(step, 0),
        )

    def gate_copy(step, slot):
        mate = flip(spot, step, team)
        return copy(
            gate_mid.at[:, mate], gate_in.at[slot], hs_sem.at[mate], hr_sem.at[slot],
            peer_at(0, step),
        )

    def part_copy(step, slot):
        mate = flip(spot, step, team)
        return copy(
            part_out.at[mate], part_in.at[slot], qs_sem.at[mate], qr_sem.at[slot],
            peer_at(0, step),
        )

    def line_copy(step, slot):
        other = flip(plane, step, PLANES)
        return copy(
            line_out.at[other], line_in.at[slot], ls_sem.at[other], lr_sem.at[slot],
            peer_at(step, 0),
        )

    def over_peers(body):
        def step(k, carry):
            body(partner(k))
            return carry

        lax.fori_loop(1, n, step, 0)

    def make_plane(half, plane_step):
        def step(k, carry):
            owner = peer_at(plane_step, k)
            prod_out[half, owner] = product(owner, half)
            return carry

        lax.fori_loop(0, team, step, 0)

    def send_plane(half, plane_step, first):
        def step(k, carry):
            prod_copy(half, peer_at(plane_step, k), me).start()
            return carry

        lax.fori_loop(first, team, step, 0)

    @pl.when(is_outer == 1)
    def _():
        pl.semaphore_wait(barrier, 2 * team - 1)
        for k in range(team):
            signal(side_in, peer_at(1, k))

    plane_loads[0].wait()
    make_plane(0, early_step(0))

    @pl.when(is_mid == 1)
    def _():
        pl.semaphore_wait(barrier, 2 * team - 1)

    send_plane(0, early_step(0), 0)
    plane_loads[1].wait()
    make_plane(0, 0)
    prod_in[0, me] = prod_out[0, me]
    send_plane(0, 0, 1)

    @pl.when(is_mid == 1)
    def _():
        pl.semaphore_wait(side_in, team)
        signal(far_side_in, peer_at(3, 0))
        signal(mids_in, peer_at(1, 0))

    plane_loads[2].wait()
    make_plane(0, early_step(2))

    @pl.when(is_outer == 1)
    def _():
        pl.semaphore_wait(mids_in, 1)

    send_plane(0, early_step(2), 0)
    plane_loads[3].wait()
    make_plane(0, early_step(3))

    pl.semaphore_wait(far_side_in, 1)

    @pl.when(is_mid == 1)
    def _():
        signal(far_side_in, peer_at(1, 0))

    send_plane(0, early_step(3), 0)
    for half in range(1, halves):
        for k in range(PLANES):
            make_plane(half, k)
        prod_in[half, me] = prod_out[half, me]

    def send_rest():
        for half in range(1, halves):
            over_peers(lambda peer, half=half: prod_copy(half, peer, me).start())

    off_load.wait()
    gate_load.wait()
    chosen = lax.broadcasted_iota(jnp.int32, (16, rows), 1) == off_ref[me]
    chosen = jnp.where(chosen, 1.0, 0.0).astype(jnp.bfloat16)

    def make_gate(peer):
        cols = pl.ds(pl.multiple_of(peer * group, LANES), group)
        return dot32(chosen, streams_ref[0, :, cols])[0:1, :].astype(GATE)

    def put_gate(peer):
        gate_out[peer] = make_gate(peer)

    over_peers(put_gate)
    put_gate(me)
    gate_mid[plane] = gate_out[pl.ds(plane * team, team)]
    for k in reversed(range(1, PLANES)):
        gate_line(k, plane).start()
    pl.when(is_mid == 1)(send_rest)

    for each in tap_loads:
        each.wait()

    def segment(d, carry):
        taps_d = filter_ref[:, pl.ds(pl.multiple_of(d * BLOCK, LANES), BLOCK)]
        dims = (((1,), (1,)), ((), ()))
        value = lax.dot_general(
            fwd_hi_ref[...], taps_d, dims, preferred_element_type=jnp.float32
        ) + lax.dot_general(fwd_lo_ref[...], taps_d, dims, preferred_element_type=jnp.float32)
        for half in range(halves):
            taps[half, d] = value[:, half * width : (half + 1) * width]
        return carry

    lax.fori_loop(0, n_blocks, segment, 0)
    row_id = lax.broadcasted_iota(jnp.int32, (BLOCK, width), 0)
    sign = jnp.where(row_id % 2 == 0, 1.0, -1.0)
    for half in range(halves):
        def window(step, carry, half=half):
            d = n_blocks - 1 - step
            re = taps[half, d, :BLOCK]
            im = taps[half, d, BLOCK:]
            taps[half, d, :BLOCK] = taps[half, d - 1, :BLOCK] + sign * im
            taps[half, d, BLOCK:] = taps[half, d - 1, BLOCK:] - sign * re
            return carry

        lax.fori_loop(0, n_blocks - 1, window, 0)
        re = taps[half, 0, :BLOCK]
        im = taps[half, 0, BLOCK:]
        taps[half, 0, :BLOCK] = sign * im
        taps[half, 0, BLOCK:] = -sign * re

    def pair_of_blocks(ref, half, first):
        both = [
            ref[half, pl.ds((first + k) * per_block, per_block)].reshape(BLOCK, width)
            for k in range(2)
        ]
        return jnp.concatenate(both, axis=1)

    for each in late_loads:
        each.wait()

    def pair_at(q):
        return flip(plane, far_step(q), PLANES)

    def send_pair(q, half):
        for k in reversed(range(team)):
            peer = pair_at(q) * team + flip(spot, k, team)

            @pl.when(peer != me)
            def _():
                filt_copy(half, peer, me).start()

    for half in range(halves):
        over_peers(lambda peer, half=half: prod_copy(half, peer, peer).wait_recv())
        if half == 0:
            pl.when(is_outer == 1)(send_rest)

        def forward(q, carry, half=half):
            x = pair_of_blocks(prod_in, half, 2 * q)
            value = dot32(fwd_hi_ref[...], x) + dot32(fwd_lo_ref[...], x)
            spec[2 * q] = value[:, :width]
            spec[2 * q + 1] = value[:, width:]
            return carry

        lax.fori_loop(0, n_blocks // 2, forward, 0)

        def mix(tile, carry, half=half):
            re_rows = pl.ds(pl.multiple_of(tile * 8, 8), 8)
            im_rows = pl.ds(pl.multiple_of(BLOCK + tile * 8, 8), 8)
            x_re = [spec[i, re_rows] for i in range(n_blocks)]
            x_im = [spec[i, im_rows] for i in range(n_blocks)]
            for i in reversed(range(n_blocks)):
                w_re = None
                for d in range(i + 1):
                    g_re, g_im = taps[half, d, re_rows], taps[half, d, im_rows]
                    a, b = x_re[i - d], x_im[i - d]
                    t_re = a * g_re - b * g_im
                    t_im = a * g_im + b * g_re
                    w_re, w_im = (t_re, t_im) if w_re is None else (w_re + t_re, w_im + t_im)
                spec[i, re_rows] = w_re
                spec[i, im_rows] = w_im
            return carry

        lax.fori_loop(0, BLOCK // 8, mix, 0)

        def inverse(q_step, carry, half=half):
            q = pair_at(q_step)
            w = jnp.concatenate([spec[2 * q], spec[2 * q + 1]], axis=1)
            w_hi = w.astype(jnp.bfloat16)
            w_lo = (w - w_hi.astype(jnp.float32)).astype(jnp.bfloat16)
            y = dot32(inv_hi_ref[...], w_hi) + (
                dot32(inv_hi_ref[...], w_lo) + dot32(inv_lo_ref[...], w_hi)
            )
            y = y.astype(jnp.bfloat16)
            for k in range(2):
                part = y[:, k * width : (k + 1) * width].reshape(per_block, rows, width)
                filt_out[half, pl.ds((2 * q + k) * per_block, per_block)] = part

            @pl.when(q_step > 0 if half < halves - 1 else q_step == 1)
            def _():
                send_pair(q_step - 1, half)

            return carry

        lax.fori_loop(0, n_blocks // 2, inverse, 0)
        if half < halves - 1:
            send_pair(n_blocks // 2 - 1, half)
        if half == max(halves - 2, 0):
            for k in range(1, PLANES):
                gate_line(k, flip(plane, k, PLANES)).wait_recv()
            gate_in[spot] = gate_mid[:, spot]
            for k in range(1, team):
                gate_copy(k, spot).start()

    def finish(owner, half, value):
        cols = lanes(owner, half)
        gate = streams_ref[0, :, cols].astype(jnp.float32)
        mixed_ref[:, cols] = (gate * value.astype(jnp.float32)).astype(jnp.bfloat16)

    for k in range(1, team):
        gate_copy(k, flip(spot, k, team)).wait_recv()
    variant = lax.broadcasted_iota(jnp.int32, (n, LANES), 0)
    place = jnp.zeros((n, LANES), jnp.int32)
    for j in range(n):
        j_rank = j % team * PLANES + j // team
        place = jnp.where(variant == j_rank, off_ref[j] + j * rows, place)
    column = lax.broadcasted_iota(jnp.int32, (n, n * rows), 1)
    pick = jnp.where(column == place[:, :1], 1.0, 0.0).astype(jnp.bfloat16)
    picked = [dot32(pick, filt_out[half].reshape(n * rows, width)) for half in range(halves)]
    picked = jnp.concatenate(picked, axis=1)
    gate_rows = gate_in[...].astype(jnp.float32).reshape(n, group)
    rows16 = (gate_rows * picked).astype(jnp.bfloat16)
    gain_rows[...] = gain_ref[...].astype(jnp.float32).reshape(1, model_width)
    gain = gain_rows[:, pl.ds(pl.multiple_of(me * group, LANES), group)]
    rows32 = rows16.astype(jnp.float32)
    weighted = (rows32 * gain).astype(jnp.bfloat16)
    raw = dot32(weighted, unembed_ref[...])
    square = jnp.sum(rows32 * rows32, axis=1, keepdims=True)
    part_out[:, :, :vocab] = raw.reshape(team, PLANES, vocab)
    part_out[:, :, vocab:] = jnp.broadcast_to(square, (n, LANES)).reshape(team, PLANES, LANES)
    part_in[spot] = part_out[spot]
    for k in range(1, team):
        part_copy(k, spot).start()
    for half in range(halves):
        finish(me, half, filt_out[half, me])
    for k in range(1, team):
        part_copy(k, flip(spot, k, team)).wait_recv()
    line_out[...] = jnp.sum(part_in[...], axis=0).reshape(PLANES, 1, vocab + LANES)
    line_in[plane] = line_out[plane]
    for k in reversed(range(1, PLANES)):
        line_copy(k, plane).start()
    for k in range(1, n_blocks // 2):
        send_pair(k, halves - 1)

    def score():
        for k in range(1, PLANES):
            line_copy(k, flip(plane, k, PLANES)).wait_recv()
        total = jnp.sum(line_in[...], axis=0)
        scale = lax.rsqrt(total[:, vocab : vocab + 1] / model_width + norm_eps)
        logits = total[:, :vocab] * scale
        largest = jnp.max(logits, axis=1, keepdims=True)
        log_total = largest + jnp.log(jnp.sum(jnp.exp(logits - largest), axis=1, keepdims=True))
        vocab_ids = lax.broadcasted_iota(jnp.int32, (1, vocab), 1)
        ref_logit = jnp.sum(
            jnp.where(vocab_ids == ref_id_ref[0], logits, 0.0), axis=1, keepdims=True
        )
        alt_logit = jnp.sum(
            jnp.where(vocab_ids == alt_id_ref[0], logits, 0.0), axis=1, keepdims=True
        )
        lane = lax.broadcasted_iota(jnp.int32, (1, 2), 1)
        scores_ref[...] = jnp.where(lane == 0, ref_logit - log_total, alt_logit - ref_logit)

    def land(half, k):
        level = k // team
        step = jnp.where(level < 2, level, far_step(level - 2))
        turn = jnp.where(level == 0, k, team - 1 - lax.rem(k, team))
        peer = peer_at(step, turn)
        filt_copy(half, peer, peer).wait_recv()
        finish(peer, half, filt_in[half, peer])

    for half in range(halves):
        def landed(k, carry, half=half):
            land(half, k)
            return carry

        last = half == halves - 1
        lax.fori_loop(1, n - team if last else n, landed, 0)
        if last:
            score()
            lax.fori_loop(n - team, n, landed, 0)

    def drain(peer):
        for half in range(halves):
            prod_copy(half, peer, me).wait_send()
            filt_copy(half, peer, me).wait_send()

    over_peers(drain)
    for k in range(1, team):
        gate_copy(k, spot).wait_send()
        part_copy(k, spot).wait_send()
    for k in range(1, PLANES):
        gate_line(k, plane).wait_send()
        line_copy(k, plane).wait_send()


def store_kernel(mixed_ref, scores_ref, mixed_hbm, scores_hbm, sem):
    share = mixed_ref.shape[0] // STORES
    moves = [pltpu.make_async_copy(scores_ref, scores_hbm, sem.at[STORES])]
    for k in range(STORES):
        part = pl.ds(k * share, share)
        moves.append(pltpu.make_async_copy(mixed_ref.at[part], mixed_hbm.at[part], sem.at[k]))
    for move in moves:
        move.start()
    for move in moves:
        move.wait()


def fused_shards(streams, long_filter, gain, unembed, offsets, ref_ids, alt_ids):
    n = lax.axis_size("seq")
    rows, model_width = streams.shape[1:]
    group = model_width // n
    team = n // PLANES
    vocab = unembed.shape[1]
    halves = group // LANES
    width = LANES
    n_blocks = n * rows // BLOCK
    cfg = (n, halves, rows, width, vocab, model_width)
    tables = [jnp.asarray(t) for t in block_tables(BLOCK)]
    vmem = pl.BlockSpec(memory_space=pltpu.VMEM)
    smem = pl.BlockSpec(memory_space=pltpu.SMEM)
    hbm = pl.BlockSpec(memory_space=pltpu.HBM)
    dma = pltpu.SemaphoreType.DMA
    block_buffer = pltpu.VMEM((halves, n, rows, width), jnp.bfloat16)
    operands = [offsets, ref_ids, alt_ids, streams, long_filter, gain, unembed] + tables
    held = [pltpu.SMEM(each.shape, each.dtype) for each in operands[:1]]
    held += [pltpu.VMEM(each.shape, each.dtype) for each in operands[3:]]
    held_out = [pltpu.with_memory_space_constraint(each, pltpu.HBM) for each in operands]
    held_out[1:3] = [ref_ids, alt_ids]
    mixed, scores = pl.pallas_call(
        functools.partial(layer_kernel, cfg),
        out_shape=(
            jax.ShapeDtypeStruct((rows, model_width), jnp.bfloat16),
            jax.ShapeDtypeStruct((1, 2), jnp.float32),
        ),
        in_specs=[hbm] + [smem] * 2 + [hbm] * (len(operands) - 3),
        out_specs=(vmem, vmem),
        scratch_shapes=held
        + [block_buffer] * 4
        + [
            pltpu.VMEM((n_blocks, 2 * BLOCK, width), jnp.float32),
            pltpu.VMEM((halves, n_blocks, 2 * BLOCK, width), jnp.float32),
            pltpu.VMEM((n, 1, group), GATE),
            pltpu.VMEM((PLANES, team, 1, group), GATE),
            pltpu.VMEM((team, PLANES, 1, group), GATE),
            pltpu.VMEM((team, PLANES, vocab + LANES), jnp.float32),
            pltpu.VMEM((team, PLANES, vocab + LANES), jnp.float32),
            pltpu.VMEM((PLANES, 1, vocab + LANES), jnp.float32),
            pltpu.VMEM((PLANES, 1, vocab + LANES), jnp.float32),
            pltpu.VMEM((1, model_width), jnp.float32),
        ]
        + [dma((halves, n))] * 4
        + [dma((PLANES,))] * 2
        + [dma((team,))] * 4
        + [dma((PLANES,))] * 2
        + [dma((13,))]
        + [pltpu.SemaphoreType.REGULAR] * 3,
        compiler_params=pltpu.CompilerParams(
            collective_id=0, has_side_effects=True, vmem_limit_bytes=48 * 2**20
        ),
    )(*held_out)
    mixed, scores = pl.pallas_call(
        store_kernel,
        out_shape=(
            jax.ShapeDtypeStruct(mixed.shape, mixed.dtype),
            jax.ShapeDtypeStruct(scores.shape, scores.dtype),
        ),
        in_specs=[vmem, vmem],
        out_specs=(hbm, hbm),
        scratch_shapes=[dma((STORES + 1,))],
    )(
        pltpu.with_memory_space_constraint(mixed, pltpu.VMEM),
        pltpu.with_memory_space_constraint(scores, pltpu.VMEM),
    )
    return (mixed, scores.T)


def shards(streams, long_filter, gain, unembed, offsets, ref_ids, alt_ids):
    n = lax.axis_size("seq")
    rows, model_width = streams.shape[1:]
    fits = (
        model_width % (n * LANES) == 0
        and BLOCK % rows == 0
        and rows % 16 == 0
        and n * rows == 2 * PLANES * BLOCK
        and n % 16 == 0
        and n & (n - 1) == 0
        and model_width // n <= 4 * LANES
        and unembed.shape[1] % LANES == 0
        and ref_ids.shape[0] == 1
        and offsets.shape[0] == n
    )
    body = fused_shards if fits else plain_shards
    return body(streams, long_filter, gain, unembed, offsets, ref_ids, alt_ids)


def solution(mesh):
    placed = (
        P(None, ("grp", "seq"), None),
        P("seq", None),
        P(),
        P("seq", None),
        P("grp"),
        P(("grp", "seq")),
        P(("grp", "seq")),
    )
    return jax.shard_map(
        shards,
        mesh=mesh,
        in_specs=placed,
        out_specs=(P(("grp", "seq"), None), P(None, ("grp", "seq"))),
        check_vma=False,
    )
```

```python
import functools
import math

import jax
import jax.numpy as jnp
import numpy as np
from jax import lax
from jax.experimental import pallas as pl
from jax.experimental.pallas import tpu as pltpu
from jax.sharding import PartitionSpec as P

norm_eps = 1e-06
highest = lax.Precision.HIGHEST
LANES = 128
BLOCK = 256
PLANES = 4
STORES = 4
GATE = jnp.bfloat16
MESH = pl.DeviceIdType.MESH


def angle_pair(left_count, right_count, period):
    product = (
        jnp.arange(left_count, dtype=jnp.int32)[:, None]
        * jnp.arange(right_count, dtype=jnp.int32)[None, :]
        % period
    )
    theta = product.astype(jnp.float32) * (2.0 * math.pi / period)
    return (jnp.cos(theta), jnp.sin(theta))


def forward_spectrum(signal, outer_cos, outer_sin, twist_cos, twist_sin, inner_cos, inner_sin):
    first_re = jnp.einsum("kn,cnm->ckm", outer_cos, signal, precision=highest)
    first_im = -jnp.einsum("kn,cnm->ckm", outer_sin, signal, precision=highest)
    middle_re = first_re * twist_cos + first_im * twist_sin
    middle_im = first_im * twist_cos - first_re * twist_sin
    spec_re = jnp.einsum("ckn,nm->ckm", middle_re, inner_cos, precision=highest) + jnp.einsum(
        "ckn,nm->ckm", middle_im, inner_sin, precision=highest
    )
    spec_im = jnp.einsum("ckn,nm->ckm", middle_im, inner_cos, precision=highest) - jnp.einsum(
        "ckn,nm->ckm", middle_re, inner_sin, precision=highest
    )
    return (spec_re, spec_im)


def causal_filter(signal_rows, kernel_rows, n_blocks):
    channels, length = signal_rows.shape
    half_rows = length // n_blocks
    outer_len = 2 * half_rows
    period = 2 * length
    outer_cos, outer_sin = angle_pair(outer_len, half_rows, outer_len)
    twist_cos, twist_sin = angle_pair(outer_len, n_blocks, period)
    inner_cos, inner_sin = angle_pair(n_blocks, n_blocks, n_blocks)
    tables = (outer_cos, outer_sin, twist_cos, twist_sin, inner_cos, inner_sin)
    signal_re, signal_im = forward_spectrum(
        signal_rows.astype(jnp.float32).reshape(channels, half_rows, n_blocks), *tables
    )
    kernel_re, kernel_im = forward_spectrum(
        kernel_rows.astype(jnp.float32).reshape(channels, half_rows, n_blocks), *tables
    )
    joint_re = signal_re * kernel_re - signal_im * kernel_im
    joint_im = signal_re * kernel_im + signal_im * kernel_re
    back_re = jnp.einsum("ckn,nm->ckm", joint_re, inner_cos, precision=highest) - jnp.einsum(
        "ckn,nm->ckm", joint_im, inner_sin, precision=highest
    )
    back_im = jnp.einsum("ckn,nm->ckm", joint_im, inner_cos, precision=highest) + jnp.einsum(
        "ckn,nm->ckm", joint_re, inner_sin, precision=highest
    )
    turned_re = back_re * twist_cos - back_im * twist_sin
    turned_im = back_im * twist_cos + back_re * twist_sin
    result = jnp.einsum("kn,ckm->cnm", outer_cos, turned_re, precision=highest) - jnp.einsum(
        "kn,ckm->cnm", outer_sin, turned_im, precision=highest
    )
    return (result / period).reshape(channels, length)


def variant_scores(raw_terms, square_terms, model_width, ref_ids, alt_ids):
    logits = raw_terms * lax.rsqrt(square_terms / model_width + norm_eps)[:, None]
    largest = jnp.max(logits, axis=1)
    log_total = largest + jnp.log(jnp.sum(jnp.exp(logits - largest[:, None]), axis=1))
    vocab_ids = jnp.arange(logits.shape[1], dtype=jnp.int32)
    ref_logit = jnp.sum(jnp.where(vocab_ids[None, :] == ref_ids[:, None], logits, 0.0), axis=1)
    alt_logit = jnp.sum(jnp.where(vocab_ids[None, :] == alt_ids[:, None], logits, 0.0), axis=1)
    return jnp.stack([ref_logit - log_total, alt_logit - ref_logit])


def pick_local(mixed, offsets, my_index, vars_dev):
    stride_rows = mixed.shape[0] // vars_dev
    local_offsets = lax.dynamic_slice_in_dim(offsets, my_index * vars_dev, vars_dev)
    row_index = jnp.arange(vars_dev, dtype=jnp.int32) * stride_rows + local_offsets
    return mixed[row_index]


def plain_shards(streams, long_filter, gain, unembed, offsets, ref_ids, alt_ids):
    n_devices = lax.axis_size("seq")
    my_index = lax.axis_index("seq")
    tok_rows = streams.shape[1]
    model_width = streams.shape[2]
    group_width = model_width // n_devices
    length = tok_rows * n_devices
    vars_dev = ref_ids.shape[0]
    products = (streams[1].astype(jnp.float32) * streams[2].astype(jnp.float32)).astype(
        jnp.bfloat16
    )
    split_view = products.reshape(tok_rows, n_devices, group_width)
    moved_prod = lax.all_to_all(split_view, "seq", split_axis=1, concat_axis=0, tiled=True)
    convolved = causal_filter(moved_prod.reshape(length, group_width).T, long_filter, n_devices)
    filtered_back = convolved.astype(jnp.bfloat16).T.reshape(length, 1, group_width)
    filtered = lax.all_to_all(
        filtered_back, "seq", split_axis=0, concat_axis=1, tiled=True
    ).reshape(tok_rows, model_width)
    mixed = (streams[0].astype(jnp.float32) * filtered.astype(jnp.float32)).astype(jnp.bfloat16)
    picked = pick_local(mixed, offsets, my_index, vars_dev)
    weighted = (picked.astype(jnp.float32) * gain.astype(jnp.float32)[None, :]).astype(jnp.bfloat16)
    square_terms = jnp.sum(jnp.square(picked.astype(jnp.float32)), axis=1)
    raw_terms = jnp.dot(
        weighted,
        lax.all_gather(unembed, "seq", axis=0, tiled=True),
        preferred_element_type=jnp.float32,
    )
    scores = variant_scores(raw_terms, square_terms, model_width, ref_ids, alt_ids)
    return (mixed, scores)


def block_tables(block):
    freq = 2 * np.arange(block)[:, None] + 1
    time = np.arange(block)[None, :]
    period = 4 * block
    theta = (freq * time % period) * (2.0 * np.pi / period)
    forward = np.concatenate([np.cos(theta), -np.sin(theta)], axis=0)
    theta = (freq * (time + block) % period).T * (2.0 * np.pi / period)
    inverse = np.concatenate([np.cos(theta), -np.sin(theta)], axis=1) / block
    split = []
    for table in (forward, inverse):
        high = table.astype(np.float32).astype(jnp.bfloat16)
        low = (table - high.astype(np.float64)).astype(np.float32).astype(jnp.bfloat16)
        split += [high, low]
    return split


def dot32(left, right):
    return jnp.dot(left, right, preferred_element_type=jnp.float32)


def layer_kernel(
    cfg,
    off_hbm, ref_id_ref, alt_id_ref,
    streams_hbm, filter_hbm, gain_hbm, unembed_hbm,
    fwd_hi_hbm, fwd_lo_hbm, inv_hi_hbm, inv_lo_hbm,
    mixed_ref, scores_ref,
    off_ref,
    streams_ref, filter_ref, gain_ref, unembed_ref,
    fwd_hi_ref, fwd_lo_ref, inv_hi_ref, inv_lo_ref,
    prod_out, prod_in, filt_out, filt_in, spec, taps,
    gate_out, gate_mid, gate_in, part_out, part_in, line_out, line_in, gain_rows,
    ps_sem, pr_sem, fs_sem, fr_sem, gs_sem, gr_sem, hs_sem, hr_sem, qs_sem, qr_sem, ls_sem, lr_sem, in_sem,
    side_in, mids_in, far_side_in,
):
    n, halves, rows, width, vocab, model_width = cfg
    me = lax.axis_index("seq")
    n_blocks = n * rows // BLOCK
    per_block = BLOCK // rows
    group = halves * width

    barrier = pltpu.get_barrier_semaphore()

    team = n // PLANES
    plane = me // team
    spot = lax.rem(me, team)
    is_mid = lax.rem((plane + 1) // 2, 2)
    is_outer = 1 - is_mid

    def flip(value, step, size):
        bit, out = 1, 0
        while bit < size:
            out = out + bit * lax.rem(value // bit + step // bit, 2)
            bit *= 2
        return out

    def peer_at(plane_step, spot_step):
        return flip(plane, plane_step, PLANES) * team + flip(spot, spot_step, team)

    def far_step(k):
        return 3 - k + jnp.where(k < 2, is_mid * (2 * k - 1), 0)

    def partner(k):
        return peer_at(far_step((k - 1) // team), team - 1 - lax.rem(k - 1, team))

    def signal(sem, peer):
        pl.semaphore_signal(sem, inc=1, device_id={"seq": peer}, device_id_type=MESH)

    def greet(plane_step, first):
        for k in range(first, team):
            signal(barrier, peer_at(plane_step, k))

    @pl.when(is_mid == 1)
    def _():
        greet(3, 0)
        greet(1, 0)

    greet(0, 1)

    def early_step(k):
        mid_steps, outer_steps = (3, 0, 1, 2), (1, 0, 2, 3)
        return outer_steps[k] + (mid_steps[k] - outer_steps[k]) * is_mid

    def plane_stream(k):
        share = model_width // PLANES
        first = pl.multiple_of(flip(plane, early_step(k), PLANES) * share, LANES)
        part = (pl.ds(1, 2), slice(None), pl.ds(first, share))
        return pltpu.make_async_copy(streams_hbm.at[part], streams_ref.at[part], in_sem.at[k])

    def load(src, dst, sem):
        return pltpu.make_async_copy(src, dst, in_sem.at[sem])

    plane_loads = [plane_stream(k) for k in range(PLANES)]
    gate_load = load(streams_hbm.at[0], streams_ref.at[0], 4)
    off_load = load(off_hbm, off_ref, 5)
    tap_loads = [
        load(filter_hbm, filter_ref, 6),
        load(fwd_hi_hbm, fwd_hi_ref, 7),
        load(fwd_lo_hbm, fwd_lo_ref, 8),
    ]
    late_loads = [
        load(inv_hi_hbm, inv_hi_ref, 9),
        load(inv_lo_hbm, inv_lo_ref, 10),
        load(gain_hbm, gain_ref, 11),
        load(unembed_hbm, unembed_ref, 12),
    ]
    for each in plane_loads + [off_load, gate_load] + tap_loads + late_loads:
        each.start()

    def lanes(owner, half):
        return pl.ds(pl.multiple_of(owner * group + half * width, LANES), width)

    def product(owner, half):
        cols = lanes(owner, half)
        left = streams_ref[1, :, cols].astype(jnp.float32)
        right = streams_ref[2, :, cols].astype(jnp.float32)
        return (left * right).astype(jnp.bfloat16)

    def copy(src, dst, send_sem, recv_sem, peer):
        return pltpu.make_async_remote_copy(
            src_ref=src, dst_ref=dst, send_sem=send_sem, recv_sem=recv_sem,
            device_id={"seq": peer}, device_id_type=MESH,
        )

    def prod_copy(half, peer, slot):
        return copy(
            prod_out.at[half, peer], prod_in.at[half, slot],
            ps_sem.at[half, peer], pr_sem.at[half, slot], peer,
        )

    def filt_copy(half, peer, slot):
        return copy(
            filt_out.at[half, peer], filt_in.at[half, slot],
            fs_sem.at[half, peer], fr_sem.at[half, slot], peer,
        )

    def gate_line(step, slot):
        other = flip(plane, step, PLANES)
        return copy(
            gate_out.at[pl.ds(other * team, team)], gate_mid.at[slot],
            gs_sem.at[other], gr_sem.at[slot], peer_at(step, 0),
        )

    def gate_copy(step, slot):
        mate = flip(spot, step, team)
        return copy(
            gate_mid.at[:, mate], gate_in.at[slot], hs_sem.at[mate], hr_sem.at[slot],
            peer_at(0, step),
        )

    def part_copy(step, slot):
        mate = flip(spot, step, team)
        return copy(
            part_out.at[mate], part_in.at[slot], qs_sem.at[mate], qr_sem.at[slot],
            peer_at(0, step),
        )

    def line_copy(step, slot):
        other = flip(plane, step, PLANES)
        return copy(
            line_out.at[other], line_in.at[slot], ls_sem.at[other], lr_sem.at[slot],
            peer_at(step, 0),
        )

    def over_peers(body):
        def step(k, carry):
            body(partner(k))
            return carry

        lax.fori_loop(1, n, step, 0)

    def make_plane(half, plane_step):
        def step(k, carry):
            owner = peer_at(plane_step, k)
            prod_out[half, owner] = product(owner, half)
            return carry

        lax.fori_loop(0, team, step, 0)

    def send_plane(half, plane_step, first):
        def step(k, carry):
            prod_copy(half, peer_at(plane_step, k), me).start()
            return carry

        lax.fori_loop(first, team, step, 0)

    @pl.when(is_outer == 1)
    def _():
        pl.semaphore_wait(barrier, 2 * team - 1)
        for k in range(team):
            signal(side_in, peer_at(1, k))

    plane_loads[0].wait()
    make_plane(0, early_step(0))

    @pl.when(is_mid == 1)
    def _():
        pl.semaphore_wait(barrier, 2 * team - 1)

    send_plane(0, early_step(0), 0)
    plane_loads[1].wait()
    make_plane(0, 0)
    prod_in[0, me] = prod_out[0, me]
    send_plane(0, 0, 1)

    @pl.when(is_mid == 1)
    def _():
        pl.semaphore_wait(side_in, team)
        signal(far_side_in, peer_at(3, 0))
        signal(mids_in, peer_at(1, 0))

    plane_loads[2].wait()
    make_plane(0, early_step(2))

    @pl.when(is_outer == 1)
    def _():
        pl.semaphore_wait(mids_in, 1)

    send_plane(0, early_step(2), 0)
    plane_loads[3].wait()
    make_plane(0, early_step(3))

    pl.semaphore_wait(far_side_in, 1)

    @pl.when(is_mid == 1)
    def _():
        signal(far_side_in, peer_at(1, 0))

    send_plane(0, early_step(3), 0)
    for half in range(1, halves):
        for k in range(PLANES):
            make_plane(half, k)
        prod_in[half, me] = prod_out[half, me]

    def send_rest():
        for half in range(1, halves):
            over_peers(lambda peer, half=half: prod_copy(half, peer, me).start())

    off_load.wait()
    gate_load.wait()
    chosen = lax.broadcasted_iota(jnp.int32, (16, rows), 1) == off_ref[me]
    chosen = jnp.where(chosen, 1.0, 0.0).astype(jnp.bfloat16)

    def make_gate(peer):
        cols = pl.ds(pl.multiple_of(peer * group, LANES), group)
        return dot32(chosen, streams_ref[0, :, cols])[0:1, :].astype(GATE)

    def put_gate(peer):
        gate_out[peer] = make_gate(peer)

    over_peers(put_gate)
    put_gate(me)
    gate_mid[plane] = gate_out[pl.ds(plane * team, team)]
    for k in reversed(range(1, PLANES)):
        gate_line(k, plane).start()
    pl.when(is_mid == 1)(send_rest)

    for each in tap_loads:
        each.wait()

    def segment(d, carry):
        taps_d = filter_ref[:, pl.ds(pl.multiple_of(d * BLOCK, LANES), BLOCK)]
        dims = (((1,), (1,)), ((), ()))
        value = lax.dot_general(
            fwd_hi_ref[...], taps_d, dims, preferred_element_type=jnp.float32
        ) + lax.dot_general(fwd_lo_ref[...], taps_d, dims, preferred_element_type=jnp.float32)
        for half in range(halves):
            taps[half, d] = value[:, half * width : (half + 1) * width]
        return carry

    lax.fori_loop(0, n_blocks, segment, 0)
    row_id = lax.broadcasted_iota(jnp.int32, (BLOCK, width), 0)
    sign = jnp.where(row_id % 2 == 0, 1.0, -1.0)
    for half in range(halves):
        def window(step, carry, half=half):
            d = n_blocks - 1 - step
            re = taps[half, d, :BLOCK]
            im = taps[half, d, BLOCK:]
            taps[half, d, :BLOCK] = taps[half, d - 1, :BLOCK] + sign * im
            taps[half, d, BLOCK:] = taps[half, d - 1, BLOCK:] - sign * re
            return carry

        lax.fori_loop(0, n_blocks - 1, window, 0)
        re = taps[half, 0, :BLOCK]
        im = taps[half, 0, BLOCK:]
        taps[half, 0, :BLOCK] = sign * im
        taps[half, 0, BLOCK:] = -sign * re

    def pair_of_blocks(ref, half, first):
        both = [
            ref[half, pl.ds((first + k) * per_block, per_block)].reshape(BLOCK, width)
            for k in range(2)
        ]
        return jnp.concatenate(both, axis=1)

    for each in late_loads:
        each.wait()

    def pair_at(q):
        return flip(plane, far_step(q), PLANES)

    def send_pair(q, half):
        for k in reversed(range(team)):
            peer = pair_at(q) * team + flip(spot, k, team)

            @pl.when(peer != me)
            def _():
                filt_copy(half, peer, me).start()

    for half in range(halves):
        over_peers(lambda peer, half=half: prod_copy(half, peer, peer).wait_recv())
        if half == 0:
            pl.when(is_outer == 1)(send_rest)

        def forward(q, carry, half=half):
            x = pair_of_blocks(prod_in, half, 2 * q)
            value = dot32(fwd_hi_ref[...], x) + dot32(fwd_lo_ref[...], x)
            spec[2 * q] = value[:, :width]
            spec[2 * q + 1] = value[:, width:]
            return carry

        lax.fori_loop(0, n_blocks // 2, forward, 0)

        def mix(tile, carry, half=half):
            re_rows = pl.ds(pl.multiple_of(tile * 8, 8), 8)
            im_rows = pl.ds(pl.multiple_of(BLOCK + tile * 8, 8), 8)
            x_re = [spec[i, re_rows] for i in range(n_blocks)]
            x_im = [spec[i, im_rows] for i in range(n_blocks)]
            for i in reversed(range(n_blocks)):
                w_re = None
                for d in range(i + 1):
                    g_re, g_im = taps[half, d, re_rows], taps[half, d, im_rows]
                    a, b = x_re[i - d], x_im[i - d]
                    t_re = a * g_re - b * g_im
                    t_im = a * g_im + b * g_re
                    w_re, w_im = (t_re, t_im) if w_re is None else (w_re + t_re, w_im + t_im)
                spec[i, re_rows] = w_re
                spec[i, im_rows] = w_im
            return carry

        lax.fori_loop(0, BLOCK // 8, mix, 0)

        def inverse(q_step, carry, half=half):
            q = pair_at(q_step)
            w = jnp.concatenate([spec[2 * q], spec[2 * q + 1]], axis=1)
            w_hi = w.astype(jnp.bfloat16)
            w_lo = (w - w_hi.astype(jnp.float32)).astype(jnp.bfloat16)
            y = dot32(inv_hi_ref[...], w_hi) + (
                dot32(inv_hi_ref[...], w_lo) + dot32(inv_lo_ref[...], w_hi)
            )
            y = y.astype(jnp.bfloat16)
            for k in range(2):
                part = y[:, k * width : (k + 1) * width].reshape(per_block, rows, width)
                filt_out[half, pl.ds((2 * q + k) * per_block, per_block)] = part

            @pl.when(q_step > 0 if half < halves - 1 else q_step == 1)
            def _():
                send_pair(q_step - 1, half)

            return carry

        lax.fori_loop(0, n_blocks // 2, inverse, 0)
        if half < halves - 1:
            send_pair(n_blocks // 2 - 1, half)
        if half == max(halves - 2, 0):
            for k in range(1, PLANES):
                gate_line(k, flip(plane, k, PLANES)).wait_recv()
            gate_in[spot] = gate_mid[:, spot]
            for k in range(1, team):
                gate_copy(k, spot).start()

    def finish(owner, half, value):
        cols = lanes(owner, half)
        gate = streams_ref[0, :, cols].astype(jnp.float32)
        mixed_ref[:, cols] = (gate * value.astype(jnp.float32)).astype(jnp.bfloat16)

    for k in range(1, team):
        gate_copy(k, flip(spot, k, team)).wait_recv()
    variant = lax.broadcasted_iota(jnp.int32, (n, LANES), 0)
    place = jnp.zeros((n, LANES), jnp.int32)
    for j in range(n):
        j_rank = j % team * PLANES + j // team
        place = jnp.where(variant == j_rank, off_ref[j] + j * rows, place)
    column = lax.broadcasted_iota(jnp.int32, (n, n * rows), 1)
    pick = jnp.where(column == place[:, :1], 1.0, 0.0).astype(jnp.bfloat16)
    picked = [dot32(pick, filt_out[half].reshape(n * rows, width)) for half in range(halves)]
    picked = jnp.concatenate(picked, axis=1)
    gate_rows = gate_in[...].astype(jnp.float32).reshape(n, group)
    rows16 = (gate_rows * picked).astype(jnp.bfloat16)
    gain_rows[...] = gain_ref[...].astype(jnp.float32).reshape(1, model_width)
    gain = gain_rows[:, pl.ds(pl.multiple_of(me * group, LANES), group)]
    rows32 = rows16.astype(jnp.float32)
    weighted = (rows32 * gain).astype(jnp.bfloat16)
    raw = dot32(weighted, unembed_ref[...])
    square = jnp.sum(rows32 * rows32, axis=1, keepdims=True)
    part_out[:, :, :vocab] = raw.reshape(team, PLANES, vocab)
    part_out[:, :, vocab:] = jnp.broadcast_to(square, (n, LANES)).reshape(team, PLANES, LANES)
    part_in[spot] = part_out[spot]
    for k in range(1, team):
        part_copy(k, spot).start()
    for half in range(halves):
        finish(me, half, filt_out[half, me])
    for k in range(1, team):
        part_copy(k, flip(spot, k, team)).wait_recv()
    line_out[...] = jnp.sum(part_in[...], axis=0).reshape(PLANES, 1, vocab + LANES)
    line_in[plane] = line_out[plane]
    for k in reversed(range(1, PLANES)):
        line_copy(k, plane).start()

    @pl.when(is_mid == 1)
    def _():
        send_pair(1, halves - 1)

    for k in range(2, n_blocks // 2):
        send_pair(k, halves - 1)

    def score():
        for k in range(1, PLANES):
            line_copy(k, flip(plane, k, PLANES)).wait_recv()
        total = jnp.sum(line_in[...], axis=0)
        scale = lax.rsqrt(total[:, vocab : vocab + 1] / model_width + norm_eps)
        logits = total[:, :vocab] * scale
        largest = jnp.max(logits, axis=1, keepdims=True)
        log_total = largest + jnp.log(jnp.sum(jnp.exp(logits - largest), axis=1, keepdims=True))
        vocab_ids = lax.broadcasted_iota(jnp.int32, (1, vocab), 1)
        ref_logit = jnp.sum(
            jnp.where(vocab_ids == ref_id_ref[0], logits, 0.0), axis=1, keepdims=True
        )
        alt_logit = jnp.sum(
            jnp.where(vocab_ids == alt_id_ref[0], logits, 0.0), axis=1, keepdims=True
        )
        lane = lax.broadcasted_iota(jnp.int32, (1, 2), 1)
        scores_ref[...] = jnp.where(lane == 0, ref_logit - log_total, alt_logit - ref_logit)

    def land(half, k):
        level = k // team
        step = jnp.where(level < 2, level, far_step(level - 2))
        turn = jnp.where(level == 0, k, team - 1 - lax.rem(k, team))
        peer = peer_at(step, turn)
        known = is_outer * (peer == release) if half == halves - 1 else 0

        @pl.when(known == 0)
        def _():
            filt_copy(half, peer, peer).wait_recv()

        finish(peer, half, filt_in[half, peer])

    release = peer_at(2, 2)
    for half in range(halves):
        def landed(k, carry, half=half):
            land(half, k)
            return carry

        last = half == halves - 1
        if last:

            @pl.when(is_outer == 1)
            def _():
                filt_copy(half, release, release).wait_recv()
                send_pair(1, half)

        lax.fori_loop(1, n - team if last else n, landed, 0)
        if last:
            score()
            lax.fori_loop(n - team, n, landed, 0)

    def drain(peer):
        for half in range(halves):
            prod_copy(half, peer, me).wait_send()
            filt_copy(half, peer, me).wait_send()

    over_peers(drain)
    for k in range(1, team):
        gate_copy(k, spot).wait_send()
        part_copy(k, spot).wait_send()
    for k in range(1, PLANES):
        gate_line(k, plane).wait_send()
        line_copy(k, plane).wait_send()


def store_kernel(mixed_ref, scores_ref, mixed_hbm, scores_hbm, sem):
    share = mixed_ref.shape[0] // STORES
    moves = [pltpu.make_async_copy(scores_ref, scores_hbm, sem.at[STORES])]
    for k in range(STORES):
        part = pl.ds(k * share, share)
        moves.append(pltpu.make_async_copy(mixed_ref.at[part], mixed_hbm.at[part], sem.at[k]))
    for move in moves:
        move.start()
    for move in moves:
        move.wait()


def fused_shards(streams, long_filter, gain, unembed, offsets, ref_ids, alt_ids):
    n = lax.axis_size("seq")
    rows, model_width = streams.shape[1:]
    group = model_width // n
    team = n // PLANES
    vocab = unembed.shape[1]
    halves = group // LANES
    width = LANES
    n_blocks = n * rows // BLOCK
    cfg = (n, halves, rows, width, vocab, model_width)
    tables = [jnp.asarray(t) for t in block_tables(BLOCK)]
    vmem = pl.BlockSpec(memory_space=pltpu.VMEM)
    smem = pl.BlockSpec(memory_space=pltpu.SMEM)
    hbm = pl.BlockSpec(memory_space=pltpu.HBM)
    dma = pltpu.SemaphoreType.DMA
    block_buffer = pltpu.VMEM((halves, n, rows, width), jnp.bfloat16)
    operands = [offsets, ref_ids, alt_ids, streams, long_filter, gain, unembed] + tables
    held = [pltpu.SMEM(each.shape, each.dtype) for each in operands[:1]]
    held += [pltpu.VMEM(each.shape, each.dtype) for each in operands[3:]]
    held_out = [pltpu.with_memory_space_constraint(each, pltpu.HBM) for each in operands]
    held_out[1:3] = [ref_ids, alt_ids]
    mixed, scores = pl.pallas_call(
        functools.partial(layer_kernel, cfg),
        out_shape=(
            jax.ShapeDtypeStruct((rows, model_width), jnp.bfloat16),
            jax.ShapeDtypeStruct((1, 2), jnp.float32),
        ),
        in_specs=[hbm] + [smem] * 2 + [hbm] * (len(operands) - 3),
        out_specs=(vmem, vmem),
        scratch_shapes=held
        + [block_buffer] * 4
        + [
            pltpu.VMEM((n_blocks, 2 * BLOCK, width), jnp.float32),
            pltpu.VMEM((halves, n_blocks, 2 * BLOCK, width), jnp.float32),
            pltpu.VMEM((n, 1, group), GATE),
            pltpu.VMEM((PLANES, team, 1, group), GATE),
            pltpu.VMEM((team, PLANES, 1, group), GATE),
            pltpu.VMEM((team, PLANES, vocab + LANES), jnp.float32),
            pltpu.VMEM((team, PLANES, vocab + LANES), jnp.float32),
            pltpu.VMEM((PLANES, 1, vocab + LANES), jnp.float32),
            pltpu.VMEM((PLANES, 1, vocab + LANES), jnp.float32),
            pltpu.VMEM((1, model_width), jnp.float32),
        ]
        + [dma((halves, n))] * 4
        + [dma((PLANES,))] * 2
        + [dma((team,))] * 4
        + [dma((PLANES,))] * 2
        + [dma((13,))]
        + [pltpu.SemaphoreType.REGULAR] * 3,
        compiler_params=pltpu.CompilerParams(
            collective_id=0, has_side_effects=True, vmem_limit_bytes=48 * 2**20
        ),
    )(*held_out)
    mixed, scores = pl.pallas_call(
        store_kernel,
        out_shape=(
            jax.ShapeDtypeStruct(mixed.shape, mixed.dtype),
            jax.ShapeDtypeStruct(scores.shape, scores.dtype),
        ),
        in_specs=[vmem, vmem],
        out_specs=(hbm, hbm),
        scratch_shapes=[dma((STORES + 1,))],
    )(
        pltpu.with_memory_space_constraint(mixed, pltpu.VMEM),
        pltpu.with_memory_space_constraint(scores, pltpu.VMEM),
    )
    return (mixed, scores.T)


def shards(streams, long_filter, gain, unembed, offsets, ref_ids, alt_ids):
    n = lax.axis_size("seq")
    rows, model_width = streams.shape[1:]
    fits = (
        model_width % (n * LANES) == 0
        and BLOCK % rows == 0
        and rows % 16 == 0
        and n * rows == 2 * PLANES * BLOCK
        and n % 16 == 0
        and n & (n - 1) == 0
        and model_width // n <= 4 * LANES
        and unembed.shape[1] % LANES == 0
        and ref_ids.shape[0] == 1
        and offsets.shape[0] == n
    )
    body = fused_shards if fits else plain_shards
    return body(streams, long_filter, gain, unembed, offsets, ref_ids, alt_ids)


def solution(mesh):
    placed = (
        P(None, ("grp", "seq"), None),
        P("seq", None),
        P(),
        P("seq", None),
        P("grp"),
        P(("grp", "seq")),
        P(("grp", "seq")),
    )
    return jax.shard_map(
        shards,
        mesh=mesh,
        in_specs=placed,
        out_specs=(P(("grp", "seq"), None), P(None, ("grp", "seq"))),
        check_vma=False,
    )
```

```python
import functools
import math

import jax
import jax.numpy as jnp
import numpy as np
from jax import lax
from jax.experimental import pallas as pl
from jax.experimental.pallas import tpu as pltpu
from jax.sharding import PartitionSpec as P

norm_eps = 1e-06
highest = lax.Precision.HIGHEST
LANES = 128
BLOCK = 256
PLANES = 4
STORES = 4
GATE = jnp.bfloat16
MESH = pl.DeviceIdType.MESH


def angle_pair(left_count, right_count, period):
    product = (
        jnp.arange(left_count, dtype=jnp.int32)[:, None]
        * jnp.arange(right_count, dtype=jnp.int32)[None, :]
        % period
    )
    theta = product.astype(jnp.float32) * (2.0 * math.pi / period)
    return (jnp.cos(theta), jnp.sin(theta))


def forward_spectrum(signal, outer_cos, outer_sin, twist_cos, twist_sin, inner_cos, inner_sin):
    first_re = jnp.einsum("kn,cnm->ckm", outer_cos, signal, precision=highest)
    first_im = -jnp.einsum("kn,cnm->ckm", outer_sin, signal, precision=highest)
    middle_re = first_re * twist_cos + first_im * twist_sin
    middle_im = first_im * twist_cos - first_re * twist_sin
    spec_re = jnp.einsum("ckn,nm->ckm", middle_re, inner_cos, precision=highest) + jnp.einsum(
        "ckn,nm->ckm", middle_im, inner_sin, precision=highest
    )
    spec_im = jnp.einsum("ckn,nm->ckm", middle_im, inner_cos, precision=highest) - jnp.einsum(
        "ckn,nm->ckm", middle_re, inner_sin, precision=highest
    )
    return (spec_re, spec_im)


def causal_filter(signal_rows, kernel_rows, n_blocks):
    channels, length = signal_rows.shape
    half_rows = length // n_blocks
    outer_len = 2 * half_rows
    period = 2 * length
    outer_cos, outer_sin = angle_pair(outer_len, half_rows, outer_len)
    twist_cos, twist_sin = angle_pair(outer_len, n_blocks, period)
    inner_cos, inner_sin = angle_pair(n_blocks, n_blocks, n_blocks)
    tables = (outer_cos, outer_sin, twist_cos, twist_sin, inner_cos, inner_sin)
    signal_re, signal_im = forward_spectrum(
        signal_rows.astype(jnp.float32).reshape(channels, half_rows, n_blocks), *tables
    )
    kernel_re, kernel_im = forward_spectrum(
        kernel_rows.astype(jnp.float32).reshape(channels, half_rows, n_blocks), *tables
    )
    joint_re = signal_re * kernel_re - signal_im * kernel_im
    joint_im = signal_re * kernel_im + signal_im * kernel_re
    back_re = jnp.einsum("ckn,nm->ckm", joint_re, inner_cos, precision=highest) - jnp.einsum(
        "ckn,nm->ckm", joint_im, inner_sin, precision=highest
    )
    back_im = jnp.einsum("ckn,nm->ckm", joint_im, inner_cos, precision=highest) + jnp.einsum(
        "ckn,nm->ckm", joint_re, inner_sin, precision=highest
    )
    turned_re = back_re * twist_cos - back_im * twist_sin
    turned_im = back_im * twist_cos + back_re * twist_sin
    result = jnp.einsum("kn,ckm->cnm", outer_cos, turned_re, precision=highest) - jnp.einsum(
        "kn,ckm->cnm", outer_sin, turned_im, precision=highest
    )
    return (result / period).reshape(channels, length)


def variant_scores(raw_terms, square_terms, model_width, ref_ids, alt_ids):
    logits = raw_terms * lax.rsqrt(square_terms / model_width + norm_eps)[:, None]
    largest = jnp.max(logits, axis=1)
    log_total = largest + jnp.log(jnp.sum(jnp.exp(logits - largest[:, None]), axis=1))
    vocab_ids = jnp.arange(logits.shape[1], dtype=jnp.int32)
    ref_logit = jnp.sum(jnp.where(vocab_ids[None, :] == ref_ids[:, None], logits, 0.0), axis=1)
    alt_logit = jnp.sum(jnp.where(vocab_ids[None, :] == alt_ids[:, None], logits, 0.0), axis=1)
    return jnp.stack([ref_logit - log_total, alt_logit - ref_logit])


def pick_local(mixed, offsets, my_index, vars_dev):
    stride_rows = mixed.shape[0] // vars_dev
    local_offsets = lax.dynamic_slice_in_dim(offsets, my_index * vars_dev, vars_dev)
    row_index = jnp.arange(vars_dev, dtype=jnp.int32) * stride_rows + local_offsets
    return mixed[row_index]


def plain_shards(streams, long_filter, gain, unembed, offsets, ref_ids, alt_ids):
    n_devices = lax.axis_size("seq")
    my_index = lax.axis_index("seq")
    tok_rows = streams.shape[1]
    model_width = streams.shape[2]
    group_width = model_width // n_devices
    length = tok_rows * n_devices
    vars_dev = ref_ids.shape[0]
    products = (streams[1].astype(jnp.float32) * streams[2].astype(jnp.float32)).astype(
        jnp.bfloat16
    )
    split_view = products.reshape(tok_rows, n_devices, group_width)
    moved_prod = lax.all_to_all(split_view, "seq", split_axis=1, concat_axis=0, tiled=True)
    convolved = causal_filter(moved_prod.reshape(length, group_width).T, long_filter, n_devices)
    filtered_back = convolved.astype(jnp.bfloat16).T.reshape(length, 1, group_width)
    filtered = lax.all_to_all(
        filtered_back, "seq", split_axis=0, concat_axis=1, tiled=True
    ).reshape(tok_rows, model_width)
    mixed = (streams[0].astype(jnp.float32) * filtered.astype(jnp.float32)).astype(jnp.bfloat16)
    picked = pick_local(mixed, offsets, my_index, vars_dev)
    weighted = (picked.astype(jnp.float32) * gain.astype(jnp.float32)[None, :]).astype(jnp.bfloat16)
    square_terms = jnp.sum(jnp.square(picked.astype(jnp.float32)), axis=1)
    raw_terms = jnp.dot(
        weighted,
        lax.all_gather(unembed, "seq", axis=0, tiled=True),
        preferred_element_type=jnp.float32,
    )
    scores = variant_scores(raw_terms, square_terms, model_width, ref_ids, alt_ids)
    return (mixed, scores)


def block_tables(block):
    freq = 2 * np.arange(block)[:, None] + 1
    time = np.arange(block)[None, :]
    period = 4 * block
    theta = (freq * time % period) * (2.0 * np.pi / period)
    forward = np.concatenate([np.cos(theta), -np.sin(theta)], axis=0)
    theta = (freq * (time + block) % period).T * (2.0 * np.pi / period)
    inverse = np.concatenate([np.cos(theta), -np.sin(theta)], axis=1) / block
    split = []
    for table in (forward, inverse):
        high = table.astype(np.float32).astype(jnp.bfloat16)
        low = (table - high.astype(np.float64)).astype(np.float32).astype(jnp.bfloat16)
        split += [high, low]
    return split


def dot32(left, right):
    return jnp.dot(left, right, preferred_element_type=jnp.float32)


def layer_kernel(
    cfg,
    off_hbm, ref_id_ref, alt_id_ref,
    streams_hbm, filter_hbm, gain_hbm, unembed_hbm,
    fwd_hi_hbm, fwd_lo_hbm, inv_hi_hbm, inv_lo_hbm,
    mixed_ref, scores_ref,
    off_ref,
    streams_ref, filter_ref, gain_ref, unembed_ref,
    fwd_hi_ref, fwd_lo_ref, inv_hi_ref, inv_lo_ref,
    prod_out, prod_in, filt_out, filt_in, spec, taps,
    gate_out, gate_mid, gate_in, part_out, part_in, line_out, line_in, gain_rows,
    ps_sem, pr_sem, fs_sem, fr_sem, gs_sem, gr_sem, hs_sem, hr_sem, qs_sem, qr_sem, ls_sem, lr_sem, in_sem,
    side_in, mids_in, far_side_in,
):
    n, halves, rows, width, vocab, model_width = cfg
    me = lax.axis_index("seq")
    n_blocks = n * rows // BLOCK
    per_block = BLOCK // rows
    group = halves * width

    barrier = pltpu.get_barrier_semaphore()

    team = n // PLANES
    plane = me // team
    spot = lax.rem(me, team)
    is_mid = lax.rem((plane + 1) // 2, 2)
    is_outer = 1 - is_mid

    def flip(value, step, size):
        bit, out = 1, 0
        while bit < size:
            out = out + bit * lax.rem(value // bit + step // bit, 2)
            bit *= 2
        return out

    def peer_at(plane_step, spot_step):
        return flip(plane, plane_step, PLANES) * team + flip(spot, spot_step, team)

    def far_step(k):
        return 3 - k + jnp.where(k < 2, is_mid * (2 * k - 1), 0)

    def partner(k):
        return peer_at(far_step((k - 1) // team), team - 1 - lax.rem(k - 1, team))

    def signal(sem, peer):
        pl.semaphore_signal(sem, inc=1, device_id={"seq": peer}, device_id_type=MESH)

    def greet(plane_step, first):
        for k in range(first, team):
            signal(barrier, peer_at(plane_step, k))

    @pl.when(is_mid == 1)
    def _():
        greet(3, 0)
        greet(1, 0)

    greet(0, 1)

    def early_step(k):
        mid_steps, outer_steps = (3, 0, 1, 2), (1, 0, 2, 3)
        return outer_steps[k] + (mid_steps[k] - outer_steps[k]) * is_mid

    def plane_stream(k):
        share = model_width // PLANES
        first = pl.multiple_of(flip(plane, early_step(k), PLANES) * share, LANES)
        part = (pl.ds(1, 2), slice(None), pl.ds(first, share))
        return pltpu.make_async_copy(streams_hbm.at[part], streams_ref.at[part], in_sem.at[k])

    def load(src, dst, sem):
        return pltpu.make_async_copy(src, dst, in_sem.at[sem])

    plane_loads = [plane_stream(k) for k in range(PLANES)]
    gate_load = load(streams_hbm.at[0], streams_ref.at[0], 4)
    off_load = load(off_hbm, off_ref, 5)
    tap_loads = [
        load(filter_hbm, filter_ref, 6),
        load(fwd_hi_hbm, fwd_hi_ref, 7),
        load(fwd_lo_hbm, fwd_lo_ref, 8),
    ]
    late_loads = [
        load(inv_hi_hbm, inv_hi_ref, 9),
        load(inv_lo_hbm, inv_lo_ref, 10),
        load(gain_hbm, gain_ref, 11),
        load(unembed_hbm, unembed_ref, 12),
    ]
    for each in plane_loads + [off_load, gate_load] + tap_loads + late_loads:
        each.start()

    def lanes(owner, half):
        return pl.ds(pl.multiple_of(owner * group + half * width, LANES), width)

    def product(owner, half):
        cols = lanes(owner, half)
        left = streams_ref[1, :, cols].astype(jnp.float32)
        right = streams_ref[2, :, cols].astype(jnp.float32)
        return (left * right).astype(jnp.bfloat16)

    def copy(src, dst, send_sem, recv_sem, peer):
        return pltpu.make_async_remote_copy(
            src_ref=src, dst_ref=dst, send_sem=send_sem, recv_sem=recv_sem,
            device_id={"seq": peer}, device_id_type=MESH,
        )

    def prod_copy(half, peer, slot):
        return copy(
            prod_out.at[half, peer], prod_in.at[half, slot],
            ps_sem.at[half, peer], pr_sem.at[half, slot], peer,
        )

    def filt_copy(half, peer, slot):
        return copy(
            filt_out.at[half, peer], filt_in.at[half, slot],
            fs_sem.at[half, peer], fr_sem.at[half, slot], peer,
        )

    def gate_line(step, slot):
        other = flip(plane, step, PLANES)
        return copy(
            gate_out.at[pl.ds(other * team, team)], gate_mid.at[slot],
            gs_sem.at[other], gr_sem.at[slot], peer_at(step, 0),
        )

    def gate_copy(step, slot):
        mate = flip(spot, step, team)
        return copy(
            gate_mid.at[:, mate], gate_in.at[slot], hs_sem.at[mate], hr_sem.at[slot],
            peer_at(0, step),
        )

    def part_copy(step, slot):
        mate = flip(spot, step, team)
        return copy(
            part_out.at[mate], part_in.at[slot], qs_sem.at[mate], qr_sem.at[slot],
            peer_at(0, step),
        )

    def line_copy(step, slot):
        other = flip(plane, step, PLANES)
        return copy(
            line_out.at[other], line_in.at[slot], ls_sem.at[other], lr_sem.at[slot],
            peer_at(step, 0),
        )

    def over_peers(body):
        def step(k, carry):
            body(partner(k))
            return carry

        lax.fori_loop(1, n, step, 0)

    def make_plane(half, plane_step):
        def step(k, carry):
            owner = peer_at(plane_step, k)
            prod_out[half, owner] = product(owner, half)
            return carry

        lax.fori_loop(0, team, step, 0)

    def send_plane(half, plane_step, first):
        def step(k, carry):
            prod_copy(half, peer_at(plane_step, k), me).start()
            return carry

        lax.fori_loop(first, team, step, 0)

    @pl.when(is_outer == 1)
    def _():
        pl.semaphore_wait(barrier, 2 * team - 1)
        for k in range(team):
            signal(side_in, peer_at(1, k))

    plane_loads[0].wait()
    make_plane(0, early_step(0))

    @pl.when(is_mid == 1)
    def _():
        pl.semaphore_wait(barrier, 2 * team - 1)

    send_plane(0, early_step(0), 0)
    plane_loads[1].wait()
    make_plane(0, 0)
    prod_in[0, me] = prod_out[0, me]
    send_plane(0, 0, 1)

    @pl.when(is_mid == 1)
    def _():
        pl.semaphore_wait(side_in, team)
        signal(far_side_in, peer_at(3, 0))
        signal(mids_in, peer_at(1, 0))

    plane_loads[2].wait()
    make_plane(0, early_step(2))

    @pl.when(is_outer == 1)
    def _():
        pl.semaphore_wait(mids_in, 1)

    send_plane(0, early_step(2), 0)
    plane_loads[3].wait()
    make_plane(0, early_step(3))

    pl.semaphore_wait(far_side_in, 1)

    @pl.when(is_mid == 1)
    def _():
        signal(far_side_in, peer_at(1, 0))

    send_plane(0, early_step(3), 0)
    for half in range(1, halves):
        for k in range(PLANES):
            make_plane(half, k)
        prod_in[half, me] = prod_out[half, me]

    def send_rest():
        for half in range(1, halves):
            over_peers(lambda peer, half=half: prod_copy(half, peer, me).start())

    off_load.wait()
    gate_load.wait()
    chosen = lax.broadcasted_iota(jnp.int32, (16, rows), 1) == off_ref[me]
    chosen = jnp.where(chosen, 1.0, 0.0).astype(jnp.bfloat16)

    def make_gate(peer):
        cols = pl.ds(pl.multiple_of(peer * group, LANES), group)
        return dot32(chosen, streams_ref[0, :, cols])[0:1, :].astype(GATE)

    def put_gate(peer):
        gate_out[peer] = make_gate(peer)

    over_peers(put_gate)
    put_gate(me)
    gate_mid[plane] = gate_out[pl.ds(plane * team, team)]
    for k in reversed(range(1, PLANES)):
        gate_line(k, plane).start()
    pl.when(is_mid == 1)(send_rest)

    for each in tap_loads:
        each.wait()

    def segment(d, carry):
        taps_d = filter_ref[:, pl.ds(pl.multiple_of(d * BLOCK, LANES), BLOCK)]
        dims = (((1,), (1,)), ((), ()))
        value = lax.dot_general(
            fwd_hi_ref[...], taps_d, dims, preferred_element_type=jnp.float32
        ) + lax.dot_general(fwd_lo_ref[...], taps_d, dims, preferred_element_type=jnp.float32)
        for half in range(halves):
            taps[half, d] = value[:, half * width : (half + 1) * width]
        return carry

    lax.fori_loop(0, n_blocks, segment, 0)
    row_id = lax.broadcasted_iota(jnp.int32, (BLOCK, width), 0)
    sign = jnp.where(row_id % 2 == 0, 1.0, -1.0)
    for half in range(halves):
        def window(step, carry, half=half):
            d = n_blocks - 1 - step
            re = taps[half, d, :BLOCK]
            im = taps[half, d, BLOCK:]
            taps[half, d, :BLOCK] = taps[half, d - 1, :BLOCK] + sign * im
            taps[half, d, BLOCK:] = taps[half, d - 1, BLOCK:] - sign * re
            return carry

        lax.fori_loop(0, n_blocks - 1, window, 0)
        re = taps[half, 0, :BLOCK]
        im = taps[half, 0, BLOCK:]
        taps[half, 0, :BLOCK] = sign * im
        taps[half, 0, BLOCK:] = -sign * re

    def pair_of_blocks(ref, half, first):
        both = [
            ref[half, pl.ds((first + k) * per_block, per_block)].reshape(BLOCK, width)
            for k in range(2)
        ]
        return jnp.concatenate(both, axis=1)

    for each in late_loads:
        each.wait()

    def pair_at(q):
        return flip(plane, far_step(q), PLANES)

    def send_pair(q, half):
        for k in reversed(range(team)):
            peer = pair_at(q) * team + flip(spot, k, team)

            @pl.when(peer != me)
            def _():
                filt_copy(half, peer, me).start()

    for half in range(halves):
        over_peers(lambda peer, half=half: prod_copy(half, peer, peer).wait_recv())
        if half == 0:
            pl.when(is_outer == 1)(send_rest)

        def forward(q, carry, half=half):
            x = pair_of_blocks(prod_in, half, 2 * q)
            value = dot32(fwd_hi_ref[...], x) + dot32(fwd_lo_ref[...], x)
            spec[2 * q] = value[:, :width]
            spec[2 * q + 1] = value[:, width:]
            return carry

        lax.fori_loop(0, n_blocks // 2, forward, 0)

        def mix(tile, carry, half=half):
            re_rows = pl.ds(pl.multiple_of(tile * 8, 8), 8)
            im_rows = pl.ds(pl.multiple_of(BLOCK + tile * 8, 8), 8)
            x_re = [spec[i, re_rows] for i in range(n_blocks)]
            x_im = [spec[i, im_rows] for i in range(n_blocks)]
            for i in reversed(range(n_blocks)):
                w_re = None
                for d in range(i + 1):
                    g_re, g_im = taps[half, d, re_rows], taps[half, d, im_rows]
                    a, b = x_re[i - d], x_im[i - d]
                    t_re = a * g_re - b * g_im
                    t_im = a * g_im + b * g_re
                    w_re, w_im = (t_re, t_im) if w_re is None else (w_re + t_re, w_im + t_im)
                spec[i, re_rows] = w_re
                spec[i, im_rows] = w_im
            return carry

        lax.fori_loop(0, BLOCK // 8, mix, 0)

        def inverse(q_step, carry, half=half):
            q = pair_at(q_step)
            w = jnp.concatenate([spec[2 * q], spec[2 * q + 1]], axis=1)
            w_hi = w.astype(jnp.bfloat16)
            w_lo = (w - w_hi.astype(jnp.float32)).astype(jnp.bfloat16)
            y = dot32(inv_hi_ref[...], w_hi) + (
                dot32(inv_hi_ref[...], w_lo) + dot32(inv_lo_ref[...], w_hi)
            )
            y = y.astype(jnp.bfloat16)
            for k in range(2):
                part = y[:, k * width : (k + 1) * width].reshape(per_block, rows, width)
                filt_out[half, pl.ds((2 * q + k) * per_block, per_block)] = part

            @pl.when(q_step > 0 if half < halves - 1 else q_step == 1)
            def _():
                send_pair(q_step - 1, half)

            return carry

        lax.fori_loop(0, n_blocks // 2, inverse, 0)
        if half < halves - 1:
            send_pair(n_blocks // 2 - 1, half)
        if half == max(halves - 2, 0):
            for k in range(1, PLANES):
                gate_line(k, flip(plane, k, PLANES)).wait_recv()
            gate_in[spot] = gate_mid[:, spot]
            for k in range(1, team):
                gate_copy(k, spot).start()

    def finish(owner, half, value):
        cols = lanes(owner, half)
        gate = streams_ref[0, :, cols].astype(jnp.float32)
        mixed_ref[:, cols] = (gate * value.astype(jnp.float32)).astype(jnp.bfloat16)

    for k in range(1, team):
        gate_copy(k, flip(spot, k, team)).wait_recv()
    variant = lax.broadcasted_iota(jnp.int32, (n, LANES), 0)
    place = jnp.zeros((n, LANES), jnp.int32)
    for j in range(n):
        j_rank = j % team * PLANES + j // team
        place = jnp.where(variant == j_rank, off_ref[j] + j * rows, place)
    column = lax.broadcasted_iota(jnp.int32, (n, n * rows), 1)
    pick = jnp.where(column == place[:, :1], 1.0, 0.0).astype(jnp.bfloat16)
    picked = [dot32(pick, filt_out[half].reshape(n * rows, width)) for half in range(halves)]
    picked = jnp.concatenate(picked, axis=1)
    gate_rows = gate_in[...].astype(jnp.float32).reshape(n, group)
    rows16 = (gate_rows * picked).astype(jnp.bfloat16)
    gain_rows[...] = gain_ref[...].astype(jnp.float32).reshape(1, model_width)
    gain = gain_rows[:, pl.ds(pl.multiple_of(me * group, LANES), group)]
    rows32 = rows16.astype(jnp.float32)
    weighted = (rows32 * gain).astype(jnp.bfloat16)
    raw = dot32(weighted, unembed_ref[...])
    square = jnp.sum(rows32 * rows32, axis=1, keepdims=True)
    part_out[:, :, :vocab] = raw.reshape(team, PLANES, vocab)
    part_out[:, :, vocab:] = jnp.broadcast_to(square, (n, LANES)).reshape(team, PLANES, LANES)
    part_in[spot] = part_out[spot]
    for k in range(1, team):
        part_copy(k, spot).start()
    for half in range(halves):
        finish(me, half, filt_out[half, me])
    for k in range(1, team):
        part_copy(k, flip(spot, k, team)).wait_recv()
    line_out[...] = jnp.sum(part_in[...], axis=0).reshape(PLANES, 1, vocab + LANES)
    line_in[plane] = line_out[plane]
    for k in reversed(range(1, PLANES)):
        line_copy(k, plane).start()

    @pl.when(is_mid == 1)
    def _():
        send_pair(1, halves - 1)

    for k in range(2, n_blocks // 2):
        send_pair(k, halves - 1)

    def score():
        for k in range(1, PLANES):
            line_copy(k, flip(plane, k, PLANES)).wait_recv()
        total = jnp.sum(line_in[...], axis=0)
        scale = lax.rsqrt(total[:, vocab : vocab + 1] / model_width + norm_eps)
        logits = total[:, :vocab] * scale
        largest = jnp.max(logits, axis=1, keepdims=True)
        log_total = largest + jnp.log(jnp.sum(jnp.exp(logits - largest), axis=1, keepdims=True))
        vocab_ids = lax.broadcasted_iota(jnp.int32, (1, vocab), 1)
        ref_logit = jnp.sum(
            jnp.where(vocab_ids == ref_id_ref[0], logits, 0.0), axis=1, keepdims=True
        )
        alt_logit = jnp.sum(
            jnp.where(vocab_ids == alt_id_ref[0], logits, 0.0), axis=1, keepdims=True
        )
        lane = lax.broadcasted_iota(jnp.int32, (1, 2), 1)
        scores_ref[...] = jnp.where(lane == 0, ref_logit - log_total, alt_logit - ref_logit)

    def land(half, k):
        level = k // team
        step = jnp.where(level < 2, level, far_step(level - 2))
        turn = jnp.where(level == 0, k, team - 1 - lax.rem(k, team))
        peer = peer_at(step, turn)
        known = is_outer * (peer == release) if half == halves - 1 else 0

        @pl.when(known == 0)
        def _():
            filt_copy(half, peer, peer).wait_recv()

        finish(peer, half, filt_in[half, peer])

    release = peer_at(2, team - 2)

    def sent(half, first, last):
        def step(k, carry):
            filt_copy(half, partner(k), me).wait_send()
            return carry

        lax.fori_loop(first, last, step, 0)

    for half in range(halves):
        def landed(k, carry, half=half):
            land(half, k)
            return carry

        last = half == halves - 1
        if last:

            @pl.when(is_outer == 1)
            def _():
                filt_copy(half, release, release).wait_recv()
                send_pair(1, half)

            for early in range(halves):
                over_peers(lambda peer, early=early: prod_copy(early, peer, me).wait_send())
            for early in range(halves - 1):
                sent(early, 1, n)
            for k in range(1, team):
                gate_copy(k, spot).wait_send()
                part_copy(k, spot).wait_send()
            for k in range(1, PLANES):
                gate_line(k, plane).wait_send()

        lax.fori_loop(1, n - team if last else n, landed, 0)
        if last:
            score()
            for k in range(1, PLANES):
                line_copy(k, plane).wait_send()
            sent(half, 1, team + 1)
            sent(half, 2 * team + 1, n)
            for k in range(n - team, n):
                land(half, k)
    for k in range(team + 1, 2 * team + 1):
        filt_copy(halves - 1, partner(k), me).wait_send()


def store_kernel(mixed_ref, scores_ref, mixed_hbm, scores_hbm, sem):
    share = mixed_ref.shape[0] // STORES
    moves = [pltpu.make_async_copy(scores_ref, scores_hbm, sem.at[STORES])]
    for k in range(STORES):
        part = pl.ds(k * share, share)
        moves.append(pltpu.make_async_copy(mixed_ref.at[part], mixed_hbm.at[part], sem.at[k]))
    for move in moves:
        move.start()
    for move in moves:
        move.wait()


def fused_shards(streams, long_filter, gain, unembed, offsets, ref_ids, alt_ids):
    n = lax.axis_size("seq")
    rows, model_width = streams.shape[1:]
    group = model_width // n
    team = n // PLANES
    vocab = unembed.shape[1]
    halves = group // LANES
    width = LANES
    n_blocks = n * rows // BLOCK
    cfg = (n, halves, rows, width, vocab, model_width)
    tables = [jnp.asarray(t) for t in block_tables(BLOCK)]
    vmem = pl.BlockSpec(memory_space=pltpu.VMEM)
    smem = pl.BlockSpec(memory_space=pltpu.SMEM)
    hbm = pl.BlockSpec(memory_space=pltpu.HBM)
    dma = pltpu.SemaphoreType.DMA
    block_buffer = pltpu.VMEM((halves, n, rows, width), jnp.bfloat16)
    operands = [offsets, ref_ids, alt_ids, streams, long_filter, gain, unembed] + tables
    held = [pltpu.SMEM(each.shape, each.dtype) for each in operands[:1]]
    held += [pltpu.VMEM(each.shape, each.dtype) for each in operands[3:]]
    held_out = [pltpu.with_memory_space_constraint(each, pltpu.HBM) for each in operands]
    held_out[1:3] = [ref_ids, alt_ids]
    mixed, scores = pl.pallas_call(
        functools.partial(layer_kernel, cfg),
        out_shape=(
            jax.ShapeDtypeStruct((rows, model_width), jnp.bfloat16),
            jax.ShapeDtypeStruct((1, 2), jnp.float32),
        ),
        in_specs=[hbm] + [smem] * 2 + [hbm] * (len(operands) - 3),
        out_specs=(vmem, vmem),
        scratch_shapes=held
        + [block_buffer] * 4
        + [
            pltpu.VMEM((n_blocks, 2 * BLOCK, width), jnp.float32),
            pltpu.VMEM((halves, n_blocks, 2 * BLOCK, width), jnp.float32),
            pltpu.VMEM((n, 1, group), GATE),
            pltpu.VMEM((PLANES, team, 1, group), GATE),
            pltpu.VMEM((team, PLANES, 1, group), GATE),
            pltpu.VMEM((team, PLANES, vocab + LANES), jnp.float32),
            pltpu.VMEM((team, PLANES, vocab + LANES), jnp.float32),
            pltpu.VMEM((PLANES, 1, vocab + LANES), jnp.float32),
            pltpu.VMEM((PLANES, 1, vocab + LANES), jnp.float32),
            pltpu.VMEM((1, model_width), jnp.float32),
        ]
        + [dma((halves, n))] * 4
        + [dma((PLANES,))] * 2
        + [dma((team,))] * 4
        + [dma((PLANES,))] * 2
        + [dma((13,))]
        + [pltpu.SemaphoreType.REGULAR] * 3,
        compiler_params=pltpu.CompilerParams(
            collective_id=0, has_side_effects=True, vmem_limit_bytes=48 * 2**20
        ),
    )(*held_out)
    mixed, scores = pl.pallas_call(
        store_kernel,
        out_shape=(
            jax.ShapeDtypeStruct(mixed.shape, mixed.dtype),
            jax.ShapeDtypeStruct(scores.shape, scores.dtype),
        ),
        in_specs=[vmem, vmem],
        out_specs=(hbm, hbm),
        scratch_shapes=[dma((STORES + 1,))],
    )(
        pltpu.with_memory_space_constraint(mixed, pltpu.VMEM),
        pltpu.with_memory_space_constraint(scores, pltpu.VMEM),
    )
    return (mixed, scores.T)


def shards(streams, long_filter, gain, unembed, offsets, ref_ids, alt_ids):
    n = lax.axis_size("seq")
    rows, model_width = streams.shape[1:]
    fits = (
        model_width % (n * LANES) == 0
        and BLOCK % rows == 0
        and rows % 16 == 0
        and n * rows == 2 * PLANES * BLOCK
        and n % 16 == 0
        and n & (n - 1) == 0
        and model_width // n <= 4 * LANES
        and unembed.shape[1] % LANES == 0
        and ref_ids.shape[0] == 1
        and offsets.shape[0] == n
    )
    body = fused_shards if fits else plain_shards
    return body(streams, long_filter, gain, unembed, offsets, ref_ids, alt_ids)


def solution(mesh):
    placed = (
        P(None, ("grp", "seq"), None),
        P("seq", None),
        P(),
        P("seq", None),
        P("grp"),
        P(("grp", "seq")),
        P(("grp", "seq")),
    )
    return jax.shard_map(
        shards,
        mesh=mesh,
        in_specs=placed,
        out_specs=(P(("grp", "seq"), None), P(None, ("grp", "seq"))),
        check_vma=False,
    )
```

```python
import functools
import math

import jax
import jax.numpy as jnp
import numpy as np
from jax import lax
from jax.experimental import pallas as pl
from jax.experimental.pallas import tpu as pltpu
from jax.sharding import PartitionSpec as P

norm_eps = 1e-06
highest = lax.Precision.HIGHEST
LANES = 128
BLOCK = 256
PLANES = 4
STORES = 4
GATE = jnp.bfloat16
MESH = pl.DeviceIdType.MESH


def angle_pair(left_count, right_count, period):
    product = (
        jnp.arange(left_count, dtype=jnp.int32)[:, None]
        * jnp.arange(right_count, dtype=jnp.int32)[None, :]
        % period
    )
    theta = product.astype(jnp.float32) * (2.0 * math.pi / period)
    return (jnp.cos(theta), jnp.sin(theta))


def forward_spectrum(signal, outer_cos, outer_sin, twist_cos, twist_sin, inner_cos, inner_sin):
    first_re = jnp.einsum("kn,cnm->ckm", outer_cos, signal, precision=highest)
    first_im = -jnp.einsum("kn,cnm->ckm", outer_sin, signal, precision=highest)
    middle_re = first_re * twist_cos + first_im * twist_sin
    middle_im = first_im * twist_cos - first_re * twist_sin
    spec_re = jnp.einsum("ckn,nm->ckm", middle_re, inner_cos, precision=highest) + jnp.einsum(
        "ckn,nm->ckm", middle_im, inner_sin, precision=highest
    )
    spec_im = jnp.einsum("ckn,nm->ckm", middle_im, inner_cos, precision=highest) - jnp.einsum(
        "ckn,nm->ckm", middle_re, inner_sin, precision=highest
    )
    return (spec_re, spec_im)


def causal_filter(signal_rows, kernel_rows, n_blocks):
    channels, length = signal_rows.shape
    half_rows = length // n_blocks
    outer_len = 2 * half_rows
    period = 2 * length
    outer_cos, outer_sin = angle_pair(outer_len, half_rows, outer_len)
    twist_cos, twist_sin = angle_pair(outer_len, n_blocks, period)
    inner_cos, inner_sin = angle_pair(n_blocks, n_blocks, n_blocks)
    tables = (outer_cos, outer_sin, twist_cos, twist_sin, inner_cos, inner_sin)
    signal_re, signal_im = forward_spectrum(
        signal_rows.astype(jnp.float32).reshape(channels, half_rows, n_blocks), *tables
    )
    kernel_re, kernel_im = forward_spectrum(
        kernel_rows.astype(jnp.float32).reshape(channels, half_rows, n_blocks), *tables
    )
    joint_re = signal_re * kernel_re - signal_im * kernel_im
    joint_im = signal_re * kernel_im + signal_im * kernel_re
    back_re = jnp.einsum("ckn,nm->ckm", joint_re, inner_cos, precision=highest) - jnp.einsum(
        "ckn,nm->ckm", joint_im, inner_sin, precision=highest
    )
    back_im = jnp.einsum("ckn,nm->ckm", joint_im, inner_cos, precision=highest) + jnp.einsum(
        "ckn,nm->ckm", joint_re, inner_sin, precision=highest
    )
    turned_re = back_re * twist_cos - back_im * twist_sin
    turned_im = back_im * twist_cos + back_re * twist_sin
    result = jnp.einsum("kn,ckm->cnm", outer_cos, turned_re, precision=highest) - jnp.einsum(
        "kn,ckm->cnm", outer_sin, turned_im, precision=highest
    )
    return (result / period).reshape(channels, length)


def variant_scores(raw_terms, square_terms, model_width, ref_ids, alt_ids):
    logits = raw_terms * lax.rsqrt(square_terms / model_width + norm_eps)[:, None]
    largest = jnp.max(logits, axis=1)
    log_total = largest + jnp.log(jnp.sum(jnp.exp(logits - largest[:, None]), axis=1))
    vocab_ids = jnp.arange(logits.shape[1], dtype=jnp.int32)
    ref_logit = jnp.sum(jnp.where(vocab_ids[None, :] == ref_ids[:, None], logits, 0.0), axis=1)
    alt_logit = jnp.sum(jnp.where(vocab_ids[None, :] == alt_ids[:, None], logits, 0.0), axis=1)
    return jnp.stack([ref_logit - log_total, alt_logit - ref_logit])


def pick_local(mixed, offsets, my_index, vars_dev):
    stride_rows = mixed.shape[0] // vars_dev
    local_offsets = lax.dynamic_slice_in_dim(offsets, my_index * vars_dev, vars_dev)
    row_index = jnp.arange(vars_dev, dtype=jnp.int32) * stride_rows + local_offsets
    return mixed[row_index]


def plain_shards(streams, long_filter, gain, unembed, offsets, ref_ids, alt_ids):
    n_devices = lax.axis_size("seq")
    my_index = lax.axis_index("seq")
    tok_rows = streams.shape[1]
    model_width = streams.shape[2]
    group_width = model_width // n_devices
    length = tok_rows * n_devices
    vars_dev = ref_ids.shape[0]
    products = (streams[1].astype(jnp.float32) * streams[2].astype(jnp.float32)).astype(
        jnp.bfloat16
    )
    split_view = products.reshape(tok_rows, n_devices, group_width)
    moved_prod = lax.all_to_all(split_view, "seq", split_axis=1, concat_axis=0, tiled=True)
    convolved = causal_filter(moved_prod.reshape(length, group_width).T, long_filter, n_devices)
    filtered_back = convolved.astype(jnp.bfloat16).T.reshape(length, 1, group_width)
    filtered = lax.all_to_all(
        filtered_back, "seq", split_axis=0, concat_axis=1, tiled=True
    ).reshape(tok_rows, model_width)
    mixed = (streams[0].astype(jnp.float32) * filtered.astype(jnp.float32)).astype(jnp.bfloat16)
    picked = pick_local(mixed, offsets, my_index, vars_dev)
    weighted = (picked.astype(jnp.float32) * gain.astype(jnp.float32)[None, :]).astype(jnp.bfloat16)
    square_terms = jnp.sum(jnp.square(picked.astype(jnp.float32)), axis=1)
    raw_terms = jnp.dot(
        weighted,
        lax.all_gather(unembed, "seq", axis=0, tiled=True),
        preferred_element_type=jnp.float32,
    )
    scores = variant_scores(raw_terms, square_terms, model_width, ref_ids, alt_ids)
    return (mixed, scores)


def block_tables(block):
    freq = 2 * np.arange(block)[:, None] + 1
    time = np.arange(block)[None, :]
    period = 4 * block
    theta = (freq * time % period) * (2.0 * np.pi / period)
    forward = np.concatenate([np.cos(theta), -np.sin(theta)], axis=0)
    theta = (freq * (time + block) % period).T * (2.0 * np.pi / period)
    inverse = np.concatenate([np.cos(theta), -np.sin(theta)], axis=1) / block
    split = []
    for table in (forward, inverse):
        high = table.astype(np.float32).astype(jnp.bfloat16)
        low = (table - high.astype(np.float64)).astype(np.float32).astype(jnp.bfloat16)
        split += [high, low]
    return split


def dot32(left, right):
    return jnp.dot(left, right, preferred_element_type=jnp.float32)


def layer_kernel(
    cfg,
    off_hbm, ref_id_ref, alt_id_ref,
    streams_hbm, filter_hbm, gain_hbm, unembed_hbm,
    fwd_hi_hbm, fwd_lo_hbm, inv_hi_hbm, inv_lo_hbm,
    mixed_ref, scores_ref,
    off_ref,
    streams_ref, filter_ref, gain_ref, unembed_ref,
    fwd_hi_ref, fwd_lo_ref, inv_hi_ref, inv_lo_ref,
    prod_out, prod_in, filt_out, filt_in, spec, taps,
    gate_out, gate_mid, gate_in, part_out, part_in, line_out, line_in, gain_rows,
    ps_sem, pr_sem, fs_sem, fr_sem, gs_sem, gr_sem, hs_sem, hr_sem, qs_sem, qr_sem, ls_sem, lr_sem, in_sem,
    side_in, mids_in, far_side_in, across_in,
):
    n, halves, rows, width, vocab, model_width = cfg
    me = lax.axis_index("seq")
    n_blocks = n * rows // BLOCK
    per_block = BLOCK // rows
    group = halves * width

    barrier = pltpu.get_barrier_semaphore()

    team = n // PLANES
    plane = me // team
    spot = lax.rem(me, team)
    is_mid = lax.rem((plane + 1) // 2, 2)
    is_outer = 1 - is_mid

    def flip(value, step, size):
        bit, out = 1, 0
        while bit < size:
            out = out + bit * lax.rem(value // bit + step // bit, 2)
            bit *= 2
        return out

    def peer_at(plane_step, spot_step):
        return flip(plane, plane_step, PLANES) * team + flip(spot, spot_step, team)

    def far_step(k):
        return 3 - k + jnp.where(k < 2, is_mid * (2 * k - 1), 0)

    def partner(k):
        return peer_at(far_step((k - 1) // team), team - 1 - lax.rem(k - 1, team))

    def signal(sem, peer):
        pl.semaphore_signal(sem, inc=1, device_id={"seq": peer}, device_id_type=MESH)

    def early_step(k):
        mid_steps, outer_steps = (3, 0, 1, 2), (1, 0, 2, 3)
        return outer_steps[k] + (mid_steps[k] - outer_steps[k]) * is_mid

    def plane_stream(k):
        share = model_width // PLANES
        first = pl.multiple_of(flip(plane, early_step(k), PLANES) * share, LANES)
        part = (pl.ds(1, 2), slice(None), pl.ds(first, share))
        return pltpu.make_async_copy(streams_hbm.at[part], streams_ref.at[part], in_sem.at[k])

    plane_loads = [plane_stream(k) for k in range(PLANES)]
    plane_loads[0].start()
    half_team = team // 2
    side = spot // half_team

    def greet(plane_step, first, last):
        for k in range(first, last):
            signal(barrier, peer_at(plane_step, k))

    greet(0, 1, half_team)

    @pl.when(is_mid == 1)
    def _():
        greet(3, 0, half_team)

        @pl.when(side == 0)
        def _():
            greet(3, half_team, team)
            greet(0, half_team, team)

        greet(1, 0, team)

    @pl.when(is_outer == 1)
    def _():
        greet(0, half_team, team)

    def load(src, dst, sem):
        return pltpu.make_async_copy(src, dst, in_sem.at[sem])

    gate_load = load(streams_hbm.at[0], streams_ref.at[0], 4)
    off_load = load(off_hbm, off_ref, 5)
    tap_loads = [
        load(filter_hbm, filter_ref, 6),
        load(fwd_hi_hbm, fwd_hi_ref, 7),
        load(fwd_lo_hbm, fwd_lo_ref, 8),
    ]
    late_loads = [
        load(inv_hi_hbm, inv_hi_ref, 9),
        load(inv_lo_hbm, inv_lo_ref, 10),
        load(gain_hbm, gain_ref, 11),
        load(unembed_hbm, unembed_ref, 12),
    ]
    for each in plane_loads[1:] + [off_load, gate_load]:
        each.start()

    def lanes(owner, half):
        return pl.ds(pl.multiple_of(owner * group + half * width, LANES), width)

    def product(owner, half):
        cols = lanes(owner, half)
        left = streams_ref[1, :, cols].astype(jnp.float32)
        right = streams_ref[2, :, cols].astype(jnp.float32)
        return (left * right).astype(jnp.bfloat16)

    def copy(src, dst, send_sem, recv_sem, peer):
        return pltpu.make_async_remote_copy(
            src_ref=src, dst_ref=dst, send_sem=send_sem, recv_sem=recv_sem,
            device_id={"seq": peer}, device_id_type=MESH,
        )

    def prod_copy(half, peer, slot):
        return copy(
            prod_out.at[half, peer], prod_in.at[half, slot],
            ps_sem.at[half, peer], pr_sem.at[half, slot], peer,
        )

    def filt_copy(half, peer, slot):
        return copy(
            filt_out.at[half, peer], filt_in.at[half, slot],
            fs_sem.at[half, peer], fr_sem.at[half, slot], peer,
        )

    def gate_line(step, slot):
        other = flip(plane, step, PLANES)
        return copy(
            gate_out.at[pl.ds(other * team, team)], gate_mid.at[slot],
            gs_sem.at[other], gr_sem.at[slot], peer_at(step, 0),
        )

    def gate_copy(step, slot):
        mate = flip(spot, step, team)
        return copy(
            gate_mid.at[:, mate], gate_in.at[slot], hs_sem.at[mate], hr_sem.at[slot],
            peer_at(0, step),
        )

    def part_copy(step, slot):
        mate = flip(spot, step, team)
        return copy(
            part_out.at[mate], part_in.at[slot], qs_sem.at[mate], qr_sem.at[slot],
            peer_at(0, step),
        )

    def line_copy(step, slot):
        other = flip(plane, step, PLANES)
        return copy(
            line_out.at[other], line_in.at[slot], ls_sem.at[other], lr_sem.at[slot],
            peer_at(step, 0),
        )

    def over_peers(body):
        def step(k, carry):
            body(partner(k))
            return carry

        lax.fori_loop(1, n, step, 0)

    def make_plane(half, plane_step):
        def step(k, carry):
            owner = peer_at(plane_step, k)
            prod_out[half, owner] = product(owner, half)
            return carry

        lax.fori_loop(0, team, step, 0)

    def send_plane(half, plane_step, first, last):
        def step(k, carry):
            prod_copy(half, peer_at(plane_step, k), me).start()
            return carry

        lax.fori_loop(first, last, step, 0)

    @pl.when(is_outer == 1)
    def _():
        pl.semaphore_wait(barrier, 2 * team - 1)
        for k in range(team):
            signal(side_in, peer_at(1, k))

    plane_loads[0].wait()
    make_plane(0, early_step(0))

    @pl.when(is_mid == 1)
    def _():
        pl.semaphore_wait(barrier, team - 1 + side * team)

        @pl.when(side == 1)
        def _():
            for k in range(half_team, team):
                signal(across_in, peer_at(3, k))
                signal(across_in, peer_at(0, k))

    send_plane(0, early_step(0), 0, half_team)

    @pl.when(is_mid * (1 - side) == 1)
    def _():
        pl.semaphore_wait(across_in, team)

    send_plane(0, early_step(0), half_team, team)
    for each in tap_loads + late_loads:
        each.start()
    plane_loads[1].wait()
    make_plane(0, 0)
    prod_in[0, me] = prod_out[0, me]
    send_plane(0, 0, 1, team)

    @pl.when(is_mid == 1)
    def _():
        pl.semaphore_wait(side_in, team)
        signal(far_side_in, peer_at(3, 0))
        signal(mids_in, peer_at(1, 0))

    plane_loads[2].wait()
    make_plane(0, early_step(2))

    @pl.when(is_outer == 1)
    def _():
        pl.semaphore_wait(mids_in, 1)

    send_plane(0, early_step(2), 0, team)
    plane_loads[3].wait()
    make_plane(0, early_step(3))

    pl.semaphore_wait(far_side_in, 1)

    @pl.when(is_mid == 1)
    def _():
        signal(far_side_in, peer_at(1, 0))

    send_plane(0, early_step(3), 0, team)
    for half in range(1, halves):
        for k in range(PLANES):
            make_plane(half, k)
        prod_in[half, me] = prod_out[half, me]

    def send_rest():
        for half in range(1, halves):
            over_peers(lambda peer, half=half: prod_copy(half, peer, me).start())

    off_load.wait()
    gate_load.wait()
    chosen = lax.broadcasted_iota(jnp.int32, (16, rows), 1) == off_ref[me]
    chosen = jnp.where(chosen, 1.0, 0.0).astype(jnp.bfloat16)

    def make_gate(peer):
        cols = pl.ds(pl.multiple_of(peer * group, LANES), group)
        return dot32(chosen, streams_ref[0, :, cols])[0:1, :].astype(GATE)

    def put_gate(peer):
        gate_out[peer] = make_gate(peer)

    over_peers(put_gate)
    put_gate(me)
    gate_mid[plane] = gate_out[pl.ds(plane * team, team)]
    for k in reversed(range(1, PLANES)):
        gate_line(k, plane).start()
    pl.when(is_mid == 1)(send_rest)

    for each in tap_loads:
        each.wait()

    def segment(d, carry):
        taps_d = filter_ref[:, pl.ds(pl.multiple_of(d * BLOCK, LANES), BLOCK)]
        dims = (((1,), (1,)), ((), ()))
        value = lax.dot_general(
            fwd_hi_ref[...], taps_d, dims, preferred_element_type=jnp.float32
        ) + lax.dot_general(fwd_lo_ref[...], taps_d, dims, preferred_element_type=jnp.float32)
        for half in range(halves):
            taps[half, d] = value[:, half * width : (half + 1) * width]
        return carry

    lax.fori_loop(0, n_blocks, segment, 0)
    row_id = lax.broadcasted_iota(jnp.int32, (BLOCK, width), 0)
    sign = jnp.where(row_id % 2 == 0, 1.0, -1.0)
    for half in range(halves):
        def window(step, carry, half=half):
            d = n_blocks - 1 - step
            re = taps[half, d, :BLOCK]
            im = taps[half, d, BLOCK:]
            taps[half, d, :BLOCK] = taps[half, d - 1, :BLOCK] + sign * im
            taps[half, d, BLOCK:] = taps[half, d - 1, BLOCK:] - sign * re
            return carry

        lax.fori_loop(0, n_blocks - 1, window, 0)
        re = taps[half, 0, :BLOCK]
        im = taps[half, 0, BLOCK:]
        taps[half, 0, :BLOCK] = sign * im
        taps[half, 0, BLOCK:] = -sign * re

    def pair_of_blocks(ref, half, first):
        both = [
            ref[half, pl.ds((first + k) * per_block, per_block)].reshape(BLOCK, width)
            for k in range(2)
        ]
        return jnp.concatenate(both, axis=1)

    for each in late_loads:
        each.wait()

    def pair_at(q):
        return flip(plane, far_step(q), PLANES)

    def send_pair(q, half):
        for k in reversed(range(team)):
            peer = pair_at(q) * team + flip(spot, k, team)

            @pl.when(peer != me)
            def _():
                filt_copy(half, peer, me).start()

    for half in range(halves):
        over_peers(lambda peer, half=half: prod_copy(half, peer, peer).wait_recv())
        if half == 0:
            pl.when(is_outer == 1)(send_rest)

        def forward(q, carry, half=half):
            x = pair_of_blocks(prod_in, half, 2 * q)
            value = dot32(fwd_hi_ref[...], x) + dot32(fwd_lo_ref[...], x)
            spec[2 * q] = value[:, :width]
            spec[2 * q + 1] = value[:, width:]
            return carry

        lax.fori_loop(0, n_blocks // 2, forward, 0)

        def mix(tile, carry, half=half):
            re_rows = pl.ds(pl.multiple_of(tile * 8, 8), 8)
            im_rows = pl.ds(pl.multiple_of(BLOCK + tile * 8, 8), 8)
            x_re = [spec[i, re_rows] for i in range(n_blocks)]
            x_im = [spec[i, im_rows] for i in range(n_blocks)]
            for i in reversed(range(n_blocks)):
                w_re = None
                for d in range(i + 1):
                    g_re, g_im = taps[half, d, re_rows], taps[half, d, im_rows]
                    a, b = x_re[i - d], x_im[i - d]
                    t_re = a * g_re - b * g_im
                    t_im = a * g_im + b * g_re
                    w_re, w_im = (t_re, t_im) if w_re is None else (w_re + t_re, w_im + t_im)
                spec[i, re_rows] = w_re
                spec[i, im_rows] = w_im
            return carry

        lax.fori_loop(0, BLOCK // 8, mix, 0)

        def inverse(q_step, carry, half=half):
            q = pair_at(q_step)
            w = jnp.concatenate([spec[2 * q], spec[2 * q + 1]], axis=1)
            w_hi = w.astype(jnp.bfloat16)
            w_lo = (w - w_hi.astype(jnp.float32)).astype(jnp.bfloat16)
            y = dot32(inv_hi_ref[...], w_hi) + (
                dot32(inv_hi_ref[...], w_lo) + dot32(inv_lo_ref[...], w_hi)
            )
            y = y.astype(jnp.bfloat16)
            for k in range(2):
                part = y[:, k * width : (k + 1) * width].reshape(per_block, rows, width)
                filt_out[half, pl.ds((2 * q + k) * per_block, per_block)] = part

            @pl.when(q_step > 0 if half < halves - 1 else q_step == 1)
            def _():
                send_pair(q_step - 1, half)

            return carry

        lax.fori_loop(0, n_blocks // 2, inverse, 0)
        if half < halves - 1:
            send_pair(n_blocks // 2 - 1, half)
        if half == max(halves - 2, 0):
            for k in range(1, PLANES):
                gate_line(k, flip(plane, k, PLANES)).wait_recv()
            gate_in[spot] = gate_mid[:, spot]
            for k in range(1, team):
                gate_copy(k, spot).start()

    def finish(owner, half, value):
        cols = lanes(owner, half)
        gate = streams_ref[0, :, cols].astype(jnp.float32)
        mixed_ref[:, cols] = (gate * value.astype(jnp.float32)).astype(jnp.bfloat16)

    for k in range(1, team):
        gate_copy(k, flip(spot, k, team)).wait_recv()
    variant = lax.broadcasted_iota(jnp.int32, (n, LANES), 0)
    place = jnp.zeros((n, LANES), jnp.int32)
    for j in range(n):
        j_rank = j % team * PLANES + j // team
        place = jnp.where(variant == j_rank, off_ref[j] + j * rows, place)
    column = lax.broadcasted_iota(jnp.int32, (n, n * rows), 1)
    pick = jnp.where(column == place[:, :1], 1.0, 0.0).astype(jnp.bfloat16)
    picked = [dot32(pick, filt_out[half].reshape(n * rows, width)) for half in range(halves)]
    picked = jnp.concatenate(picked, axis=1)
    gate_rows = gate_in[...].astype(jnp.float32).reshape(n, group)
    rows16 = (gate_rows * picked).astype(jnp.bfloat16)
    gain_rows[...] = gain_ref[...].astype(jnp.float32).reshape(1, model_width)
    gain = gain_rows[:, pl.ds(pl.multiple_of(me * group, LANES), group)]
    rows32 = rows16.astype(jnp.float32)
    weighted = (rows32 * gain).astype(jnp.bfloat16)
    raw = dot32(weighted, unembed_ref[...])
    square = jnp.sum(rows32 * rows32, axis=1, keepdims=True)
    part_out[:, :, :vocab] = raw.reshape(team, PLANES, vocab)
    part_out[:, :, vocab:] = jnp.broadcast_to(square, (n, LANES)).reshape(team, PLANES, LANES)
    part_in[spot] = part_out[spot]
    for k in range(1, team):
        part_copy(k, spot).start()
    for half in range(halves):
        finish(me, half, filt_out[half, me])
    for k in range(1, team):
        part_copy(k, flip(spot, k, team)).wait_recv()
    line_out[...] = jnp.sum(part_in[...], axis=0).reshape(PLANES, 1, vocab + LANES)
    line_in[plane] = line_out[plane]
    for k in reversed(range(1, PLANES)):
        line_copy(k, plane).start()

    @pl.when(is_mid == 1)
    def _():
        send_pair(1, halves - 1)

    for k in range(2, n_blocks // 2):
        send_pair(k, halves - 1)

    def score():
        for k in range(1, PLANES):
            line_copy(k, flip(plane, k, PLANES)).wait_recv()
        total = jnp.sum(line_in[...], axis=0)
        scale = lax.rsqrt(total[:, vocab : vocab + 1] / model_width + norm_eps)
        logits = total[:, :vocab] * scale
        largest = jnp.max(logits, axis=1, keepdims=True)
        log_total = largest + jnp.log(jnp.sum(jnp.exp(logits - largest), axis=1, keepdims=True))
        vocab_ids = lax.broadcasted_iota(jnp.int32, (1, vocab), 1)
        ref_logit = jnp.sum(
            jnp.where(vocab_ids == ref_id_ref[0], logits, 0.0), axis=1, keepdims=True
        )
        alt_logit = jnp.sum(
            jnp.where(vocab_ids == alt_id_ref[0], logits, 0.0), axis=1, keepdims=True
        )
        lane = lax.broadcasted_iota(jnp.int32, (1, 2), 1)
        scores_ref[...] = jnp.where(lane == 0, ref_logit - log_total, alt_logit - ref_logit)

    def land(half, k):
        level = k // team
        step = jnp.where(level < 2, level, far_step(level - 2))
        turn = jnp.where(level == 0, k, team - 1 - lax.rem(k, team))
        peer = peer_at(step, turn)
        known = is_outer * (peer == release) if half == halves - 1 else 0

        @pl.when(known == 0)
        def _():
            filt_copy(half, peer, peer).wait_recv()

        finish(peer, half, filt_in[half, peer])

    release = peer_at(2, team - 2)

    def sent(half, first, last):
        def step(k, carry):
            filt_copy(half, partner(k), me).wait_send()
            return carry

        lax.fori_loop(first, last, step, 0)

    for half in range(halves):
        def landed(k, carry, half=half):
            land(half, k)
            return carry

        last = half == halves - 1
        if last:

            @pl.when(is_outer == 1)
            def _():
                filt_copy(half, release, release).wait_recv()
                send_pair(1, half)

            for early in range(halves):
                over_peers(lambda peer, early=early: prod_copy(early, peer, me).wait_send())
            for early in range(halves - 1):
                sent(early, 1, n)
            for k in range(1, team):
                gate_copy(k, spot).wait_send()
                part_copy(k, spot).wait_send()
            for k in range(1, PLANES):
                gate_line(k, plane).wait_send()

        lax.fori_loop(1, n - team if last else n, landed, 0)
        if last:
            score()
            for k in range(1, PLANES):
                line_copy(k, plane).wait_send()
            sent(half, 1, team + 1)
            sent(half, 2 * team + 1, n)
            for k in range(n - team, n):
                land(half, k)
    for k in range(team + 1, 2 * team + 1):
        filt_copy(halves - 1, partner(k), me).wait_send()


def store_kernel(mixed_ref, scores_ref, mixed_hbm, scores_hbm, sem):
    share = mixed_ref.shape[0] // STORES
    moves = [pltpu.make_async_copy(scores_ref, scores_hbm, sem.at[STORES])]
    for k in range(STORES):
        part = pl.ds(k * share, share)
        moves.append(pltpu.make_async_copy(mixed_ref.at[part], mixed_hbm.at[part], sem.at[k]))
    for move in moves:
        move.start()
    for move in moves:
        move.wait()


def fused_shards(streams, long_filter, gain, unembed, offsets, ref_ids, alt_ids):
    n = lax.axis_size("seq")
    rows, model_width = streams.shape[1:]
    group = model_width // n
    team = n // PLANES
    vocab = unembed.shape[1]
    halves = group // LANES
    width = LANES
    n_blocks = n * rows // BLOCK
    cfg = (n, halves, rows, width, vocab, model_width)
    tables = [jnp.asarray(t) for t in block_tables(BLOCK)]
    vmem = pl.BlockSpec(memory_space=pltpu.VMEM)
    smem = pl.BlockSpec(memory_space=pltpu.SMEM)
    hbm = pl.BlockSpec(memory_space=pltpu.HBM)
    dma = pltpu.SemaphoreType.DMA
    block_buffer = pltpu.VMEM((halves, n, rows, width), jnp.bfloat16)
    operands = [offsets, ref_ids, alt_ids, streams, long_filter, gain, unembed] + tables
    held = [pltpu.SMEM(each.shape, each.dtype) for each in operands[:1]]
    held += [pltpu.VMEM(each.shape, each.dtype) for each in operands[3:]]
    held_out = [pltpu.with_memory_space_constraint(each, pltpu.HBM) for each in operands]
    held_out[1:3] = [ref_ids, alt_ids]
    mixed, scores = pl.pallas_call(
        functools.partial(layer_kernel, cfg),
        out_shape=(
            jax.ShapeDtypeStruct((rows, model_width), jnp.bfloat16),
            jax.ShapeDtypeStruct((1, 2), jnp.float32),
        ),
        in_specs=[hbm] + [smem] * 2 + [hbm] * (len(operands) - 3),
        out_specs=(vmem, vmem),
        scratch_shapes=held
        + [block_buffer] * 4
        + [
            pltpu.VMEM((n_blocks, 2 * BLOCK, width), jnp.float32),
            pltpu.VMEM((halves, n_blocks, 2 * BLOCK, width), jnp.float32),
            pltpu.VMEM((n, 1, group), GATE),
            pltpu.VMEM((PLANES, team, 1, group), GATE),
            pltpu.VMEM((team, PLANES, 1, group), GATE),
            pltpu.VMEM((team, PLANES, vocab + LANES), jnp.float32),
            pltpu.VMEM((team, PLANES, vocab + LANES), jnp.float32),
            pltpu.VMEM((PLANES, 1, vocab + LANES), jnp.float32),
            pltpu.VMEM((PLANES, 1, vocab + LANES), jnp.float32),
            pltpu.VMEM((1, model_width), jnp.float32),
        ]
        + [dma((halves, n))] * 4
        + [dma((PLANES,))] * 2
        + [dma((team,))] * 4
        + [dma((PLANES,))] * 2
        + [dma((13,))]
        + [pltpu.SemaphoreType.REGULAR] * 4,
        compiler_params=pltpu.CompilerParams(
            collective_id=0, has_side_effects=True, vmem_limit_bytes=48 * 2**20
        ),
    )(*held_out)
    mixed, scores = pl.pallas_call(
        store_kernel,
        out_shape=(
            jax.ShapeDtypeStruct(mixed.shape, mixed.dtype),
            jax.ShapeDtypeStruct(scores.shape, scores.dtype),
        ),
        in_specs=[vmem, vmem],
        out_specs=(hbm, hbm),
        scratch_shapes=[dma((STORES + 1,))],
    )(
        pltpu.with_memory_space_constraint(mixed, pltpu.VMEM),
        pltpu.with_memory_space_constraint(scores, pltpu.VMEM),
    )
    return (mixed, scores.T)


def shards(streams, long_filter, gain, unembed, offsets, ref_ids, alt_ids):
    n = lax.axis_size("seq")
    rows, model_width = streams.shape[1:]
    fits = (
        model_width % (n * LANES) == 0
        and BLOCK % rows == 0
        and rows % 16 == 0
        and n * rows == 2 * PLANES * BLOCK
        and n % 16 == 0
        and n & (n - 1) == 0
        and model_width // n <= 4 * LANES
        and unembed.shape[1] % LANES == 0
        and ref_ids.shape[0] == 1
        and offsets.shape[0] == n
    )
    body = fused_shards if fits else plain_shards
    return body(streams, long_filter, gain, unembed, offsets, ref_ids, alt_ids)


def solution(mesh):
    placed = (
        P(None, ("grp", "seq"), None),
        P("seq", None),
        P(),
        P("seq", None),
        P("grp"),
        P(("grp", "seq")),
        P(("grp", "seq")),
    )
    return jax.shard_map(
        shards,
        mesh=mesh,
        in_specs=placed,
        out_specs=(P(("grp", "seq"), None), P(None, ("grp", "seq"))),
        check_vma=False,
    )
```
